512 devices in a mesh: replica: 64 (over x, y, core), tensor: 8 (over z).
Axes of the slice: x: 4, y: 8, z: 8, core: 2. Of those that a mesh axis runs over, the one named last changes fastest.
Arguments:
- features: bfloat16 [4096, 4, 7680], P('replica', None, 'tensor'), may hold values from -6 to 6
- kv_weight: bfloat16 [7680, 8, 256], P('tensor'), may hold values from -0.0625 to 0.0625
- image_owner: int32 [4096], replicated, may hold values from 0 to 63, as said below
- image_request: int32 [4096], replicated, may hold values from 0 to 7, as said below
- cross_query: bfloat16 [512, 64, 128], P('replica', 'tensor'), may hold values from -6 to 6
- self_query: bfloat16 [512, 64, 128], P('replica', 'tensor'), may hold values from -2.5 to 2.5
- self_cache: bfloat16 [512, 128, 8, 256], P('replica', None, 'tensor'), may hold values from -2.5 to 2.5
- fresh_key_value: bfloat16 [512, 8, 256], P('replica', 'tensor'), may hold values from -2.5 to 2.5
- cache_len: int32 [512], P('replica'), may hold values from 1 to 128, 32768 in all
Outputs:
- cross_out: bfloat16 [512, 64, 128], P('replica', 'tensor')
- self_out: bfloat16 [512, 64, 128], P('replica', 'tensor')
The draws below stay inside these ranges and needn't reach their ends.
Inputs may be any that keep to these rules, and one draw needn't show every extreme that they name: `image_owner`: within each aligned block of 64 consecutive images (the images of one replica group), no decode replica owns more than 2 images, and one decode replica owns exactly 2 images in every block. `image_request`: some requests have no image.
All inputs are finite; a program needn't handle non-finite values. No bound on the sum of `cache_len` on one device may be relied on, other than what follows from the above.
Results may differ from the reference program's by a relative error of at most 0.02.
Values may be sent and summed in bfloat16 or wider, within the bound.
No kernel may reach another device: no remote copies, remote signals or barrier semaphores. Data moves between devices by JAX's collectives and lax.ppermute only.
A program may use at most 64 MiB of HBM per device.

```python
import math
import jax
import jax.numpy as jnp
import numpy as np
from jax import lax

VW = 7680
HEADS = 64
KVH = 8
HEAD_SIZE = 128
IMG_ENC = 64
PATCHES = 4
REQ = 8
CACHE = 128
CAP = 2
IMAGE_TOTAL = 4096
REQS = 512
N_REPLICA = 64
N_TENSOR = 8


def owner_table(key):
    key_hot, key_blocks = jax.random.split(jax.random.fold_in(key, 71))
    hot = jax.random.randint(key_hot, (), 0, N_REPLICA).astype(jnp.int32)

    def one_block(block_key):
        key_perm, key_shuffle = jax.random.split(block_key)
        perm = jax.random.permutation(key_perm, N_REPLICA * CAP).astype(jnp.int32)
        dests = perm % N_REPLICA
        is_hot = (dests == hot).astype(jnp.int32)
        order = jnp.argsort(is_hot, stable=True)
        others = dests[order][:IMG_ENC - CAP]
        chosen = jnp.concatenate([jnp.full((CAP,), hot, jnp.int32), others])
        return chosen[jax.random.permutation(key_shuffle, IMG_ENC)]
    keys = jax.random.split(key_blocks, N_REPLICA)
    return jax.vmap(one_block)(keys).reshape(IMAGE_TOTAL).astype(jnp.int32)


def draw_image_owner(key, part):
    return owner_table(key)


def draw_image_request(key, part):
    owners = owner_table(key)
    key_perm, key_empty, key_some, key_every = jax.random.split(jax.random.fold_in(key, 73), 4)
    perm = jax.random.permutation(key_perm, N_REPLICA).astype(jnp.int32)
    flagged = (perm < N_REPLICA // 2).astype(jnp.int32)
    empty = jax.random.randint(key_empty, (N_REPLICA,), 0, REQ).astype(jnp.int32)
    some = jax.random.randint(key_some, (IMAGE_TOTAL,), 0, REQ - 1).astype(jnp.int32)
    every = jax.random.randint(key_every, (IMAGE_TOTAL,), 0, REQ).astype(jnp.int32)
    empty_image = empty[owners]
    flag_image = flagged[owners]
    skipped = some + (some >= empty_image).astype(jnp.int32)
    return jnp.where(flag_image > 0, skipped, every).astype(jnp.int32)


def level_of(key, dims, cuts, least, largest):
    def one(axis_at, blocks):
        heights = jax.random.uniform(jax.random.fold_in(jax.random.fold_in(key, 6), axis_at), (blocks,), jnp.float32, least / len(cuts), largest / len(cuts))
        return jnp.repeat(jnp.exp(heights), dims[axis_at] // blocks).reshape((-1,) + (1,) * (len(dims) - axis_at - 1))

    level = one(*cuts[0])
    for cut in cuts[1:]:
        level = level * one(*cut)
    return level


def split_up(number_of, total, reach, skew):
    weights = [(1 << 20) // math.isqrt(grade ** skew) + 1 for grade in range(2, number_of + 1)]
    spare, given = total - reach - (number_of - 1), [1] * (number_of - 1)
    while spare > 0:
        free = [i for i in range(number_of - 1) if given[i] < reach]
        pool, budget = sum([weights[i] for i in free]), spare
        for i in free:
            more = min(reach - given[i], max(1, budget * weights[i] // pool), spare)
            given[i] = given[i] + more
            spare = spare - more
    return np.array([reach] + given)


def ragged(stream_key, count, total, bound, slope):
    if count == 2:
        one = jax.random.randint(stream_key, (), max(1, total - bound), min(bound, total - 1) + 1)
        return jnp.stack([one, total - one])
    tallies = jnp.asarray(split_up(count, total, bound, slope), jnp.int32)
    couples = (count - 1) // 2
    donor, taker = tallies[1:1 + 2 * couples:2], tallies[2:2 + 2 * couples:2]
    room = jnp.minimum(donor - 1, bound - taker)
    shifted = jax.random.randint(jax.random.fold_in(stream_key, 1), (couples,), 0, 1 << 20) % (room + 1)
    tallies = tallies.at[1:1 + 2 * couples:2].set(donor - shifted).at[2:2 + 2 * couples:2].set(taker + shifted)
    return tallies[jax.random.permutation(jax.random.fold_in(stream_key, 2), count)]


def noise(key, dims, spread, bound, shards=(), held_as=jnp.bfloat16):
    drawn = spread * jax.random.normal(key, dims, jnp.float32)
    if shards:
        drawn = drawn * level_of(key, dims, shards, -0.22, 0.18)
    return jnp.clip(drawn, -bound, bound).astype(held_as)


def setup_inputs(seed: int = 0) -> dict:
    arg_keys = jax.random.split(jax.random.key(seed), 10)
    return {
        "features": noise(arg_keys[0], (IMAGE_TOTAL, PATCHES, VW), 1.0, 6.0, ((0, 64), (2, 8))),
        "kv_weight": noise(arg_keys[1], (VW, KVH, 2 * HEAD_SIZE), VW ** -0.5, 0.0625, ((0, 8),)),
        "image_owner": draw_image_owner(jax.random.fold_in(arg_keys[9], 71), 0),
        "image_request": draw_image_request(jax.random.fold_in(arg_keys[9], 71), 0),
        "cross_query": noise(arg_keys[4], (REQS, HEADS, HEAD_SIZE), 1.0, 6.0, ((0, 64), (1, 8))),
        "self_query": noise(arg_keys[5], (REQS, HEADS, HEAD_SIZE), 1.0, 2.5, ((0, 64), (1, 8))),
        "self_cache": noise(arg_keys[6], (REQS, CACHE, KVH, 2 * HEAD_SIZE), 1.0, 2.5, ((0, 64), (2, 8))),
        "fresh_key_value": noise(arg_keys[7], (REQS, KVH, 2 * HEAD_SIZE), 1.0, 2.5, ((0, 64), (1, 8))),
        "cache_len": ragged(arg_keys[8], REQS, REQS * CACHE // 2, CACHE, 2).astype(jnp.int32),
    }


def reference(features, kv_weight, image_owner, image_request, cross_query, self_query, self_cache, fresh_key_value, cache_len):
    block = VW // N_TENSOR
    rows = features.reshape(IMAGE_TOTAL * PATCHES, VW)
    weight_flat = kv_weight.reshape(VW, KVH * 2 * HEAD_SIZE)
    score_scale = 1.0 / math.sqrt(HEAD_SIZE)

    def add_block(j, total):
        cols = lax.dynamic_slice_in_dim(rows, j * block, block, 1)
        wrows = lax.dynamic_slice_in_dim(weight_flat, j * block, block, 0)
        part = jnp.dot(cols, wrows, preferred_element_type=jnp.float32).astype(jnp.bfloat16)
        part = lax.optimization_barrier(part)
        return total + part.astype(jnp.float32)
    summed = lax.fori_loop(0, N_TENSOR, add_block, jnp.zeros((IMAGE_TOTAL * PATCHES, KVH * 2 * HEAD_SIZE), jnp.float32))
    image_kv = summed.astype(jnp.bfloat16).reshape(IMAGE_TOTAL, PATCHES, KVH, 2 * HEAD_SIZE)
    unscaled_keys = image_kv[..., :HEAD_SIZE].astype(jnp.float32)
    image_keys = (unscaled_keys * lax.rsqrt(lax.optimization_barrier(jnp.mean(unscaled_keys * unscaled_keys, axis=-1, keepdims=True)) + 1e-05)).astype(jnp.bfloat16)
    image_values = image_kv[..., HEAD_SIZE:]
    order = jnp.argsort(image_owner, stable=True).astype(jnp.int32)
    owner_ids = jnp.arange(N_REPLICA, dtype=jnp.int32)
    counts = lax.optimization_barrier(jnp.sum((image_owner[None, :] == owner_ids[:, None]).astype(jnp.int32), axis=1, dtype=jnp.int32))
    starts = (jnp.cumsum(counts, dtype=jnp.int32) - counts).astype(jnp.int32)
    most = N_REPLICA * CAP
    padded = jnp.concatenate([order, jnp.zeros((most,), jnp.int32)])
    group = HEADS // KVH
    queries = cross_query.reshape(N_REPLICA, REQ, KVH, group, HEAD_SIZE)
    slots = jnp.arange(most, dtype=jnp.int32)
    req_ids = jnp.arange(REQ, dtype=jnp.int32)

    def one_owner(owner):
        idx = lax.dynamic_slice_in_dim(padded, starts[owner], most).astype(jnp.int32)
        valid = slots < counts[owner]
        keys = image_keys[idx].astype(jnp.float32)
        values = image_values[idx].astype(jnp.float32)
        req = image_request[idx]
        mask = valid[None, :] & (req[None, :] == req_ids[:, None])
        query = queries[owner].astype(jnp.float32)
        scores = jnp.einsum('bkgd,ipkd->bkgip', query, keys) * score_scale
        weight = jnp.where(mask[:, None, None, :, None], jnp.exp(scores), jnp.float32(0.0))
        total = lax.optimization_barrier(jnp.sum(weight, axis=(3, 4)))
        rounded = lax.optimization_barrier(weight.astype(jnp.bfloat16))
        numer = jnp.einsum('bkgip,ipkd->bkgd', rounded.astype(jnp.float32), values)
        has_image = jnp.any(mask, axis=1)
        safe = jnp.where(has_image[:, None, None], total, jnp.float32(1.0))
        result = jnp.where(has_image[:, None, None, None], numer / safe[..., None], jnp.float32(0.0))
        return result.astype(jnp.bfloat16)
    cross_out = lax.map(one_owner, owner_ids).reshape(REQS, HEADS, HEAD_SIZE)
    self_query_rows = self_query.reshape(REQS, KVH, group, HEAD_SIZE).astype(jnp.float32)
    cache_keys = self_cache[..., :HEAD_SIZE].astype(jnp.float32)
    cache_values = self_cache[..., HEAD_SIZE:].astype(jnp.float32)
    scores = jnp.einsum('bkgd,bskd->bkgs', self_query_rows, cache_keys) * score_scale
    live = jnp.arange(CACHE, dtype=jnp.int32)[None, :] < cache_len[:, None]
    weight = jnp.where(live[:, None, None, :], jnp.exp(scores), jnp.float32(0.0))
    fresh_weight = jnp.exp(jnp.einsum('ptwe,pte->ptw', self_query_rows, fresh_key_value[..., :HEAD_SIZE].astype(jnp.float32)) * score_scale)
    total = lax.optimization_barrier(jnp.sum(weight, axis=-1)) + fresh_weight
    rounded = lax.optimization_barrier(weight.astype(jnp.bfloat16))
    new_rounded = lax.optimization_barrier(fresh_weight.astype(jnp.bfloat16))
    numer = jnp.einsum('bkgs,bskd->bkgd', rounded.astype(jnp.float32), cache_values)
    numer = numer + new_rounded.astype(jnp.float32)[..., None] * fresh_key_value[:, :, None, HEAD_SIZE:].astype(jnp.float32)
    self_out = (numer / total[..., None]).astype(jnp.bfloat16).reshape(REQS, HEADS, HEAD_SIZE)
    return (cross_out, self_out)
```

```python
import math

import jax
import jax.numpy as jnp
from jax import lax
from jax.sharding import PartitionSpec as P


def local(
    features,
    kv_weight,
    image_owner,
    image_request,
    cross_query,
    self_query,
    self_cache,
    fresh_key_value,
    cache_len,
):
    n_rep = lax.axis_size("replica")
    n_ten = lax.axis_size("tensor")
    me_rep = lax.axis_index("replica")
    images, patches, block = features.shape
    kvh_all, width2 = kv_weight.shape[1:]
    head_width = width2 // 2
    score_scale = 1.0 / math.sqrt(head_width)
    slot_cap = max(2, 2 * images // n_rep)
    slot_all = n_rep * slot_cap
    rows = images * patches
    req_count, sq_heads, _ = self_query.shape
    kvh_local = self_cache.shape[2]
    group = sq_heads // kvh_local

    flat = features.reshape(rows, block)
    partial = lax.dot_general(
        flat, kv_weight, (((1,), (0,)), ((), ())), preferred_element_type=jnp.float32
    ).astype(jnp.bfloat16)
    partial = jnp.transpose(partial, (1, 0, 2))
    shares = lax.all_to_all(partial, "tensor", split_axis=0, concat_axis=0, tiled=True)
    shares = shares.reshape(n_ten, kvh_local * rows, width2)
    image_kv = jnp.sum(shares.astype(jnp.float32), axis=0).astype(jnp.bfloat16)

    owners = image_owner.reshape(n_rep, images)
    requests = image_request.reshape(n_rep, images)
    own_block = lax.dynamic_index_in_dim(owners, me_rep, 0, keepdims=False)
    positions = jnp.arange(images, dtype=jnp.int32)
    same_owner = own_block[:, None] == own_block[None, :]
    earlier = positions[:, None] > positions[None, :]
    rank = jnp.sum((same_owner & earlier).astype(jnp.int32), axis=1, dtype=jnp.int32)
    slot = own_block * slot_cap + rank
    row_slot = (slot[:, None] * patches + jnp.arange(patches, dtype=jnp.int32)[None, :]).reshape(rows)
    placing = (
        jnp.arange(slot_all * patches, dtype=jnp.int32)[:, None] == row_slot[None, :]
    ).astype(jnp.bfloat16)
    outgoing = jnp.dot(placing, image_kv, preferred_element_type=jnp.float32).astype(jnp.bfloat16)
    outgoing = outgoing.reshape(n_rep, slot_cap * patches, width2)
    arrived = lax.all_to_all(outgoing, "replica", split_axis=0, concat_axis=0, tiled=True)
    image_kv = arrived.reshape(slot_all * patches, kvh_local, width2)

    self_query_rows = self_query.reshape(req_count, kvh_local, group, head_width)
    scores = (
        jnp.einsum(
            "bkgd,bskd->bkgs",
            self_query_rows,
            self_cache[..., :head_width],
            preferred_element_type=jnp.float32,
        )
        * score_scale
    )
    live = jnp.arange(self_cache.shape[1], dtype=jnp.int32)[None, :] < cache_len[:, None]
    weight = jnp.where(live[:, None, None, :], jnp.exp(scores), jnp.float32(0.0))
    fresh_weight = jnp.exp(
        jnp.einsum(
            "ptwe,pte->ptw",
            self_query_rows,
            fresh_key_value[..., :head_width],
            preferred_element_type=jnp.float32,
        )
        * score_scale
    )
    total = jnp.sum(weight, axis=-1) + fresh_weight
    numer = jnp.einsum(
        "bkgs,bskd->bkgd",
        weight.astype(jnp.bfloat16),
        self_cache[..., head_width:],
        preferred_element_type=jnp.float32,
    )
    numer = numer + fresh_weight.astype(jnp.bfloat16).astype(jnp.float32)[
        ..., None
    ] * fresh_key_value[:, :, None, head_width:].astype(jnp.float32)
    self_out = (
        (numer / total[..., None]).astype(jnp.bfloat16).reshape(req_count, sq_heads, head_width)
    )

    owner_match = (owners == me_rep).astype(jnp.int32)
    rank_all = jnp.cumsum(owner_match, axis=1, dtype=jnp.int32) - owner_match
    slot_ids = jnp.arange(slot_cap, dtype=jnp.int32)
    chosen = owner_match[:, None, :] * (rank_all[:, None, :] == slot_ids[None, :, None]).astype(
        jnp.int32
    )
    slot_live = jnp.sum(chosen, axis=-1, dtype=jnp.int32)
    slot_req = jnp.sum(chosen * requests[:, None, :], axis=-1, dtype=jnp.int32)
    slot_tag = jnp.where(slot_live > 0, slot_req, -1)
    row_tag = jnp.broadcast_to(slot_tag[:, :, None], (n_rep, slot_cap, patches)).reshape(
        slot_all * patches
    )
    unscaled_keys = image_kv[..., :head_width].astype(jnp.float32)
    image_keys = (
        unscaled_keys
        * lax.rsqrt(jnp.mean(unscaled_keys * unscaled_keys, axis=-1, keepdims=True) + 1e-05)
    ).astype(jnp.bfloat16)
    image_values = image_kv[..., head_width:]
    cquery = cross_query.reshape(req_count, kvh_local, group, head_width)
    cscores = (
        jnp.einsum("bkgd,skd->bkgs", cquery, image_keys, preferred_element_type=jnp.float32)
        * score_scale
    )
    mask = row_tag[None, :] == jnp.arange(req_count, dtype=jnp.int32)[:, None]
    cweight = jnp.where(mask[:, None, None, :], jnp.exp(cscores), jnp.float32(0.0))
    ctotal = jnp.sum(cweight, axis=-1)
    cnumer = jnp.einsum(
        "bkgs,skd->bkgd",
        cweight.astype(jnp.bfloat16),
        image_values,
        preferred_element_type=jnp.float32,
    )
    has_image = jnp.any(mask, axis=1)
    safe = jnp.where(has_image[:, None, None], ctotal, jnp.float32(1.0))
    cross_out = jnp.where(
        has_image[:, None, None, None], cnumer / safe[..., None], jnp.float32(0.0)
    )
    cross_out = cross_out.astype(jnp.bfloat16).reshape(req_count, sq_heads, head_width)
    return (cross_out, self_out)


def solution(mesh):
    return jax.shard_map(
        local,
        mesh=mesh,
        in_specs=(
            P("replica", None, "tensor"),
            P("tensor", None, None),
            P(),
            P(),
            P("replica", "tensor", None),
            P("replica", "tensor", None),
            P("replica", None, "tensor", None),
            P("replica", "tensor", None),
            P("replica"),
        ),
        out_specs=(P("replica", "tensor", None), P("replica", "tensor", None)),
        check_vma=False,
    )
```

```python
import math

import jax
import jax.numpy as jnp
from jax import lax
from jax.experimental.layout import Layout, with_layout_constraint
from jax.sharding import PartitionSpec as P


def local(
    features,
    kv_weight,
    image_owner,
    image_request,
    cross_query,
    self_query,
    self_cache,
    fresh_key_value,
    cache_len,
):
    n_rep = lax.axis_size("replica")
    n_ten = lax.axis_size("tensor")
    me_rep = lax.axis_index("replica")
    images, patches, block = features.shape
    kvh_all, width2 = kv_weight.shape[1:]
    head_width = width2 // 2
    score_scale = 1.0 / math.sqrt(head_width)
    slot_cap = max(2, 2 * images // n_rep)
    slot_all = n_rep * slot_cap
    rows = images * patches
    req_count, sq_heads, _ = self_query.shape
    kvh_local = self_cache.shape[2]
    group = sq_heads // kvh_local

    me_ten = lax.axis_index("tensor")
    parity = me_ten % 2
    half = me_ten // 2
    flat = features.reshape(rows, block)
    quarter = kvh_all // 2

    def project(lhs):
        part = lax.dot_general(
            lhs, kv_weight, (((1,), (0,)), ((), ())), preferred_element_type=jnp.float32
        ).astype(jnp.bfloat16)
        part = with_layout_constraint(jnp.transpose(part, (1, 0, 2)), Layout((0, 1, 2)))
        return part.reshape(quarter, 2, lhs.shape[0], width2)

    def pick(part, index):
        return lax.dynamic_index_in_dim(part, index, 1, keepdims=False)

    neighbours = []
    for r in range(n_rep):
        for z in range(n_ten):
            step = 1 if (z + r) % 2 == 0 else -1
            neighbours.append((r * n_ten + z, r * n_ten + (z + step) % n_ten))
    both = ("replica", "tensor")
    pairs = []
    ahead = None
    for lo in range(0, rows, rows // 2):
        lhs = flat[lo : lo + rows // 2]
        if ahead is not None:
            lhs, _ = lax.optimization_barrier((lhs, ahead))
        part = project(lhs)
        ahead = pick(part, 1 - parity)
        pairs.append((pick(part, parity), lax.ppermute(ahead, both, neighbours)))
    pair = jnp.concatenate(
        [kept.astype(jnp.float32) + got.astype(jnp.float32) for kept, got in pairs], axis=1
    )
    image_kv = lax.dynamic_index_in_dim(pair, half, 0, keepdims=False)
    pair = with_layout_constraint(pair.astype(jnp.bfloat16), Layout((0, 1, 2)))
    arrivals = []
    for step in (1, quarter - 1, 2):
        outward = lax.dynamic_index_in_dim(pair, (half + step) % quarter, 0, keepdims=False)
        arrivals.append(
            lax.ppermute(outward, "tensor", [(z, (z + 2 * step) % n_ten) for z in range(n_ten)])
        )
    for arrival in arrivals:
        image_kv = image_kv + arrival.astype(jnp.float32)
    image_kv = image_kv.astype(jnp.bfloat16)

    owners = image_owner.reshape(n_rep, images)
    requests = image_request.reshape(n_rep, images)
    own_block = lax.dynamic_index_in_dim(owners, me_rep, 0, keepdims=False)
    positions = jnp.arange(images, dtype=jnp.int32)
    same_owner = own_block[:, None] == own_block[None, :]
    earlier = positions[:, None] > positions[None, :]
    rank = jnp.sum((same_owner & earlier).astype(jnp.int32), axis=1, dtype=jnp.int32)
    slot = own_block * slot_cap + rank
    row_slot = (slot[:, None] * patches + jnp.arange(patches, dtype=jnp.int32)[None, :]).reshape(rows)
    placing = (
        jnp.arange(slot_all * patches, dtype=jnp.int32)[:, None] == row_slot[None, :]
    ).astype(jnp.bfloat16)
    placing = lax.optimization_barrier(placing)
    outgoing = jnp.dot(placing, image_kv, preferred_element_type=jnp.float32).astype(jnp.bfloat16)
    outgoing = outgoing.reshape(n_rep, slot_cap * patches, width2)
    arrived = lax.all_to_all(outgoing, "replica", split_axis=0, concat_axis=0, tiled=True)
    image_kv = arrived.reshape(slot_all * patches, kvh_local, width2)

    self_query_rows = self_query.reshape(req_count, kvh_local, group, head_width)
    scores = (
        jnp.einsum(
            "bkgd,bskd->bkgs",
            self_query_rows,
            self_cache[..., :head_width],
            preferred_element_type=jnp.float32,
        )
        * score_scale
    )
    live = jnp.arange(self_cache.shape[1], dtype=jnp.int32)[None, :] < cache_len[:, None]
    weight = jnp.where(live[:, None, None, :], jnp.exp(scores), jnp.float32(0.0))
    fresh_weight = jnp.exp(
        jnp.einsum(
            "ptwe,pte->ptw",
            self_query_rows,
            fresh_key_value[..., :head_width],
            preferred_element_type=jnp.float32,
        )
        * score_scale
    )
    total = jnp.sum(weight, axis=-1) + fresh_weight
    numer = jnp.einsum(
        "bkgs,bskd->bkgd",
        weight.astype(jnp.bfloat16),
        self_cache[..., head_width:],
        preferred_element_type=jnp.float32,
    )
    numer = numer + fresh_weight.astype(jnp.bfloat16).astype(jnp.float32)[
        ..., None
    ] * fresh_key_value[:, :, None, head_width:].astype(jnp.float32)
    self_out = (
        (numer / total[..., None]).astype(jnp.bfloat16).reshape(req_count, sq_heads, head_width)
    )

    owner_match = (owners == me_rep).astype(jnp.int32)
    rank_all = jnp.cumsum(owner_match, axis=1, dtype=jnp.int32) - owner_match
    slot_ids = jnp.arange(slot_cap, dtype=jnp.int32)
    chosen = owner_match[:, None, :] * (rank_all[:, None, :] == slot_ids[None, :, None]).astype(
        jnp.int32
    )
    slot_live = jnp.sum(chosen, axis=-1, dtype=jnp.int32)
    slot_req = jnp.sum(chosen * requests[:, None, :], axis=-1, dtype=jnp.int32)
    slot_tag = jnp.where(slot_live > 0, slot_req, -1)
    row_tag = jnp.broadcast_to(slot_tag[:, :, None], (n_rep, slot_cap, patches)).reshape(
        slot_all * patches
    )
    unscaled_keys = image_kv[..., :head_width].astype(jnp.float32)
    image_keys = (
        unscaled_keys
        * lax.rsqrt(jnp.mean(unscaled_keys * unscaled_keys, axis=-1, keepdims=True) + 1e-05)
    ).astype(jnp.bfloat16)
    image_values = image_kv[..., head_width:]
    cquery = cross_query.reshape(req_count, kvh_local, group, head_width)
    cscores = (
        jnp.einsum("bkgd,skd->bkgs", cquery, image_keys, preferred_element_type=jnp.float32)
        * score_scale
    )
    mask = row_tag[None, :] == jnp.arange(req_count, dtype=jnp.int32)[:, None]
    cweight = jnp.where(mask[:, None, None, :], jnp.exp(cscores), jnp.float32(0.0))
    ctotal = jnp.sum(cweight, axis=-1)
    cnumer = jnp.einsum(
        "bkgs,skd->bkgd",
        cweight.astype(jnp.bfloat16),
        image_values,
        preferred_element_type=jnp.float32,
    )
    has_image = jnp.any(mask, axis=1)
    safe = jnp.where(has_image[:, None, None], ctotal, jnp.float32(1.0))
    cross_out = jnp.where(
        has_image[:, None, None, None], cnumer / safe[..., None], jnp.float32(0.0)
    )
    cross_out = cross_out.astype(jnp.bfloat16).reshape(req_count, sq_heads, head_width)
    return (cross_out, self_out)


def solution(mesh):
    return jax.shard_map(
        local,
        mesh=mesh,
        in_specs=(
            P("replica", None, "tensor"),
            P("tensor", None, None),
            P(),
            P(),
            P("replica", "tensor", None),
            P("replica", "tensor", None),
            P("replica", None, "tensor", None),
            P("replica", "tensor", None),
            P("replica"),
        ),
        out_specs=(P("replica", "tensor", None), P("replica", "tensor", None)),
        check_vma=False,
    )
```

```python
import math

import jax
import jax.numpy as jnp
from jax import lax
from jax.experimental.layout import Layout, with_layout_constraint
from jax.sharding import PartitionSpec as P


def local(
    features,
    kv_weight,
    image_owner,
    image_request,
    cross_query,
    self_query,
    self_cache,
    fresh_key_value,
    cache_len,
):
    n_rep = lax.axis_size("replica")
    n_ten = lax.axis_size("tensor")
    me_rep = lax.axis_index("replica")
    images, patches, block = features.shape
    kvh_all, width2 = kv_weight.shape[1:]
    head_width = width2 // 2
    score_scale = 1.0 / math.sqrt(head_width)
    slot_cap = max(2, 2 * images // n_rep)
    slot_all = n_rep * slot_cap
    rows = images * patches
    req_count, sq_heads, _ = self_query.shape
    kvh_local = self_cache.shape[2]
    group = sq_heads // kvh_local

    me_ten = lax.axis_index("tensor")
    parity = me_ten % 2
    half = me_ten // 2
    flat = features.reshape(rows, block)
    quarter = kvh_all // 2

    def project(lhs):
        part = lax.dot_general(
            lhs, kv_weight, (((1,), (0,)), ((), ())), preferred_element_type=jnp.float32
        ).astype(jnp.bfloat16)
        part = with_layout_constraint(jnp.transpose(part, (1, 0, 2)), Layout((0, 1, 2)))
        return part.reshape(quarter, 2, lhs.shape[0], width2)

    def pick(part, index):
        return lax.dynamic_index_in_dim(part, index, 1, keepdims=False)

    neighbours = []
    for r in range(n_rep):
        for z in range(n_ten):
            step = 1 if (z + r) % 2 == 0 else -1
            neighbours.append((r * n_ten + z, r * n_ten + (z + step) % n_ten))
    both = ("replica", "tensor")
    part = project(flat)
    got = lax.ppermute(pick(part, 1 - parity), both, neighbours)
    pair = pick(part, parity).astype(jnp.float32) + got.astype(jnp.float32)
    image_kv = lax.dynamic_index_in_dim(pair, half, 0, keepdims=False)
    pair = with_layout_constraint(pair.astype(jnp.bfloat16), Layout((0, 1, 2)))
    arrivals = []
    for step in (2, 1, quarter - 1):
        outward = lax.dynamic_index_in_dim(pair, (half + step) % quarter, 0, keepdims=False)
        arrivals.append(
            lax.ppermute(outward, "tensor", [(z, (z + 2 * step) % n_ten) for z in range(n_ten)])
        )
    for arrival in arrivals:
        image_kv = image_kv + arrival.astype(jnp.float32)
    image_kv = image_kv.astype(jnp.bfloat16)

    owners = image_owner.reshape(n_rep, images)
    requests = image_request.reshape(n_rep, images)
    own_block = lax.dynamic_index_in_dim(owners, me_rep, 0, keepdims=False)
    positions = jnp.arange(images, dtype=jnp.int32)
    same_owner = own_block[:, None] == own_block[None, :]
    earlier = positions[:, None] > positions[None, :]
    rank = jnp.sum((same_owner & earlier).astype(jnp.int32), axis=1, dtype=jnp.int32)
    slot = own_block * slot_cap + rank
    row_slot = (slot[:, None] * patches + jnp.arange(patches, dtype=jnp.int32)[None, :]).reshape(rows)
    placing = (
        jnp.arange(slot_all * patches, dtype=jnp.int32)[:, None] == row_slot[None, :]
    ).astype(jnp.bfloat16)
    placing = lax.optimization_barrier(placing)
    outgoing = jnp.dot(placing, image_kv, preferred_element_type=jnp.float32).astype(jnp.bfloat16)
    outgoing = outgoing.reshape(n_rep, slot_cap * patches, width2)
    arrived = lax.all_to_all(outgoing, "replica", split_axis=0, concat_axis=0, tiled=True)
    image_kv = arrived.reshape(slot_all * patches, kvh_local, width2)

    self_query_rows = self_query.reshape(req_count, kvh_local, group, head_width)
    scores = (
        jnp.einsum(
            "bkgd,bskd->bkgs",
            self_query_rows,
            self_cache[..., :head_width],
            preferred_element_type=jnp.float32,
        )
        * score_scale
    )
    live = jnp.arange(self_cache.shape[1], dtype=jnp.int32)[None, :] < cache_len[:, None]
    weight = jnp.where(live[:, None, None, :], jnp.exp(scores), jnp.float32(0.0))
    fresh_weight = jnp.exp(
        jnp.einsum(
            "ptwe,pte->ptw",
            self_query_rows,
            fresh_key_value[..., :head_width],
            preferred_element_type=jnp.float32,
        )
        * score_scale
    )
    total = jnp.sum(weight, axis=-1) + fresh_weight
    numer = jnp.einsum(
        "bkgs,bskd->bkgd",
        weight.astype(jnp.bfloat16),
        self_cache[..., head_width:],
        preferred_element_type=jnp.float32,
    )
    numer = numer + fresh_weight.astype(jnp.bfloat16).astype(jnp.float32)[
        ..., None
    ] * fresh_key_value[:, :, None, head_width:].astype(jnp.float32)
    self_out = (
        (numer / total[..., None]).astype(jnp.bfloat16).reshape(req_count, sq_heads, head_width)
    )

    owner_match = (owners == me_rep).astype(jnp.int32)
    rank_all = jnp.cumsum(owner_match, axis=1, dtype=jnp.int32) - owner_match
    slot_ids = jnp.arange(slot_cap, dtype=jnp.int32)
    chosen = owner_match[:, None, :] * (rank_all[:, None, :] == slot_ids[None, :, None]).astype(
        jnp.int32
    )
    slot_live = jnp.sum(chosen, axis=-1, dtype=jnp.int32)
    slot_req = jnp.sum(chosen * requests[:, None, :], axis=-1, dtype=jnp.int32)
    slot_tag = jnp.where(slot_live > 0, slot_req, -1)
    row_tag = jnp.broadcast_to(slot_tag[:, :, None], (n_rep, slot_cap, patches)).reshape(
        slot_all * patches
    )
    unscaled_keys = image_kv[..., :head_width].astype(jnp.float32)
    image_keys = (
        unscaled_keys
        * lax.rsqrt(jnp.mean(unscaled_keys * unscaled_keys, axis=-1, keepdims=True) + 1e-05)
    ).astype(jnp.bfloat16)
    image_values = image_kv[..., head_width:]
    cquery = cross_query.reshape(req_count, kvh_local, group, head_width)
    cscores = (
        jnp.einsum("bkgd,skd->bkgs", cquery, image_keys, preferred_element_type=jnp.float32)
        * score_scale
    )
    mask = row_tag[None, :] == jnp.arange(req_count, dtype=jnp.int32)[:, None]
    cweight = jnp.where(mask[:, None, None, :], jnp.exp(cscores), jnp.float32(0.0))
    ctotal = jnp.sum(cweight, axis=-1)
    cnumer = jnp.einsum(
        "bkgs,skd->bkgd",
        cweight.astype(jnp.bfloat16),
        image_values,
        preferred_element_type=jnp.float32,
    )
    has_image = jnp.any(mask, axis=1)
    safe = jnp.where(has_image[:, None, None], ctotal, jnp.float32(1.0))
    cross_out = jnp.where(
        has_image[:, None, None, None], cnumer / safe[..., None], jnp.float32(0.0)
    )
    cross_out = cross_out.astype(jnp.bfloat16).reshape(req_count, sq_heads, head_width)
    return (cross_out, self_out)


def solution(mesh):
    return jax.shard_map(
        local,
        mesh=mesh,
        in_specs=(
            P("replica", None, "tensor"),
            P("tensor", None, None),
            P(),
            P(),
            P("replica", "tensor", None),
            P("replica", "tensor", None),
            P("replica", None, "tensor", None),
            P("replica", "tensor", None),
            P("replica"),
        ),
        out_specs=(P("replica", "tensor", None), P("replica", "tensor", None)),
        check_vma=False,
    )
```

```python
import math

import jax
import jax.numpy as jnp
from jax import lax
from jax.experimental import pallas as pl
from jax.experimental.pallas import tpu as pltpu
from jax.sharding import PartitionSpec as P


CHUNKS = 4


def project_body(order_ref, features_ref, weight_ref, out_a, out_b, raw, wide, feat, flat, sem):
    block = weight_ref.shape[0]
    step = block // CHUNKS
    loads = [pltpu.make_async_copy(features_ref, feat, sem.at[CHUNKS])]
    for k in range(CHUNKS):
        part = pl.ds(k * step, step)
        loads.append(pltpu.make_async_copy(weight_ref.at[part], raw.at[part], sem.at[k]))
    for load in loads:
        load.start()
    loads[0].wait()
    flat[...] = feat[...].reshape(flat.shape)
    for k in range(CHUNKS):
        loads[k + 1].wait()
        part = pl.ds(k * step, step)
        wide[:, part, :] = jnp.swapaxes(raw[part], 0, 1)
    count = out_a.shape[0]
    for i in range(2 * count):
        product = jnp.dot(flat[...], wide[order_ref[i]], preferred_element_type=jnp.float32)
        if i < count:
            out_a[i] = product.astype(jnp.bfloat16)
        else:
            out_b[i - count] = product.astype(jnp.bfloat16)


def project(order, features, weight):
    images, patches, block = features.shape
    heads, width = weight.shape[1:]
    rows = images * patches
    count = order.shape[0] // 2
    whole = pl.BlockSpec(memory_space=pltpu.VMEM)
    return pl.pallas_call(
        project_body,
        in_specs=[
            pl.BlockSpec(memory_space=pltpu.SMEM),
            pl.BlockSpec(memory_space=pltpu.HBM),
            pl.BlockSpec(memory_space=pltpu.HBM),
        ],
        out_specs=(whole, whole),
        out_shape=(
            jax.ShapeDtypeStruct((count, rows, width), jnp.bfloat16),
            jax.ShapeDtypeStruct((count, rows, width), jnp.bfloat16),
        ),
        scratch_shapes=[
            pltpu.VMEM((block, heads, width), jnp.bfloat16),
            pltpu.VMEM((heads, block, width), jnp.bfloat16),
            pltpu.VMEM((images, patches, block), jnp.bfloat16),
            pltpu.VMEM((rows, block), jnp.bfloat16),
            pltpu.SemaphoreType.DMA((CHUNKS + 1,)),
        ],
        compiler_params=pltpu.CompilerParams(vmem_limit_bytes=32 << 20),
        cost_estimate=pl.CostEstimate(
            flops=4 * count * rows * block * width,
            bytes_accessed=2 * (block * heads * width + rows * block),
            transcendentals=0,
        ),
    )(
        order,
        pltpu.with_memory_space_constraint(features, pltpu.HBM),
        pltpu.with_memory_space_constraint(weight, pltpu.HBM),
    )


def place_body(slot_ref, kept_ref, got_ref, a_ref, b_ref, c_ref, out_ref):
    own = kept_ref[1].astype(jnp.float32) + got_ref[1].astype(jnp.float32)
    for ref in (a_ref, b_ref, c_ref):
        own = own + ref[...].astype(jnp.float32)
    slots = lax.broadcasted_iota(jnp.int32, (out_ref.shape[0], own.shape[0]), 0)
    placing = (slots == slot_ref[...]).astype(jnp.float32).astype(jnp.bfloat16)
    out_ref[...] = jnp.dot(
        placing, own.astype(jnp.bfloat16), preferred_element_type=jnp.float32
    ).astype(jnp.bfloat16)


def place(row_slot, kept, got, arrivals, slot_rows):
    rows, width = arrivals[0].shape
    operands = (row_slot.reshape(1, rows), kept, got, *arrivals)
    whole = pl.BlockSpec(memory_space=pltpu.VMEM)
    return pl.pallas_call(
        place_body,
        in_specs=[whole] * len(operands),
        out_specs=whole,
        out_shape=jax.ShapeDtypeStruct((slot_rows, width), jnp.bfloat16),
    )(*[pltpu.with_memory_space_constraint(x, pltpu.VMEM) for x in operands])


def attend_body(tag_ref, query_ref, kv_ref, out_ref):
    count, group, head_width = query_ref.shape
    slot_rows = kv_ref.shape[0]
    scale = 1.0 / math.sqrt(head_width)
    raw = kv_ref[:, :head_width].astype(jnp.float32)
    keys = (
        raw * lax.rsqrt(jnp.mean(raw * raw, axis=-1, keepdims=True) + 1e-05)
    ).astype(jnp.bfloat16)
    query = query_ref[...].reshape(count * group, head_width)
    scores = lax.dot_general(
        query, keys, (((1,), (1,)), ((), ())), preferred_element_type=jnp.float32
    )
    request = lax.broadcasted_iota(jnp.int32, (count * group, slot_rows), 0) // group
    mask = request == tag_ref[...]
    weight = jnp.where(mask, jnp.exp(scores * scale), 0.0)
    total = jnp.sum(weight, axis=-1, keepdims=True)
    present = jnp.max(mask.astype(jnp.float32), axis=-1, keepdims=True) > 0.0
    numer = jnp.dot(
        weight.astype(jnp.bfloat16), kv_ref[:, head_width:], preferred_element_type=jnp.float32
    )
    result = jnp.where(present, numer / jnp.where(present, total, 1.0), 0.0)
    out_ref[...] = result.astype(jnp.bfloat16).reshape(out_ref.shape)


def attend(row_tag, query, kv):
    operands = (row_tag.reshape(1, kv.shape[0]), query, kv)
    return pl.pallas_call(
        attend_body,
        in_specs=[pl.BlockSpec(memory_space=pltpu.VMEM)] * 3,
        out_shape=jax.ShapeDtypeStruct(query.shape, jnp.bfloat16),
    )(*[pltpu.with_memory_space_constraint(x, pltpu.VMEM) for x in operands])


def local(
    features,
    kv_weight,
    image_owner,
    image_request,
    cross_query,
    self_query,
    self_cache,
    fresh_key_value,
    cache_len,
):
    n_rep = lax.axis_size("replica")
    n_ten = lax.axis_size("tensor")
    me_rep = lax.axis_index("replica")
    images, patches, block = features.shape
    kvh_all, width2 = kv_weight.shape[1:]
    head_width = width2 // 2
    score_scale = 1.0 / math.sqrt(head_width)
    slot_cap = max(2, 2 * images // n_rep)
    slot_all = n_rep * slot_cap
    rows = images * patches
    req_count, sq_heads, _ = self_query.shape
    kvh_local = self_cache.shape[2]
    group = sq_heads // kvh_local

    me_ten = lax.axis_index("tensor")
    quarter = kvh_all // 2
    apart = jnp.array([2, 1, quarter - 1, 0], jnp.int32)
    mate = (me_ten + jnp.where((me_ten + me_rep) % 2 == 0, 1, n_ten - 1)) % n_ten
    order_out = ((mate // 2 + apart) % quarter) * 2 + mate % 2
    order_in = ((me_ten // 2 + apart) % quarter) * 2 + me_ten % 2
    neighbours = []
    for r in range(n_rep):
        for z in range(n_ten):
            step = 1 if (z + r) % 2 == 0 else -1
            neighbours.append((r * n_ten + z, r * n_ten + (z + step) % n_ten))
    both = ("replica", "tensor")
    sent_a, sent_b = project(order_out, features, kv_weight)
    got_a = lax.ppermute(sent_a, both, neighbours)
    got_b = lax.ppermute(sent_b, both, neighbours)
    order_in, _ = lax.optimization_barrier((order_in, sent_a))
    kept_a, kept_b = project(order_in, features, kv_weight)
    pair_a = (kept_a.astype(jnp.float32) + got_a.astype(jnp.float32)).astype(jnp.bfloat16)
    pair_b = (kept_b[0].astype(jnp.float32) + got_b[0].astype(jnp.float32)).astype(jnp.bfloat16)
    arrivals = [
        lax.ppermute(outward, "tensor", [(z, (z + 2 * step) % n_ten) for z in range(n_ten)])
        for outward, step in ((pair_a[0], 2), (pair_a[1], 1), (pair_b, quarter - 1))
    ]

    owners = image_owner.reshape(n_rep, images)
    requests = image_request.reshape(n_rep, images)
    own_block = lax.dynamic_index_in_dim(owners, me_rep, 0, keepdims=False)
    positions = jnp.arange(images, dtype=jnp.int32)
    same_owner = own_block[:, None] == own_block[None, :]
    earlier = positions[:, None] > positions[None, :]
    rank = jnp.sum((same_owner & earlier).astype(jnp.int32), axis=1, dtype=jnp.int32)
    slot = own_block * slot_cap + rank
    row_slot = (slot[:, None] * patches + jnp.arange(patches, dtype=jnp.int32)[None, :]).reshape(rows)
    outgoing = place(row_slot, kept_b, got_b, arrivals, slot_all * patches)
    outgoing = outgoing.reshape(n_rep, slot_cap * patches, width2)
    arrived = lax.all_to_all(outgoing, "replica", split_axis=0, concat_axis=0, tiled=True)

    self_query_rows = self_query.reshape(req_count, kvh_local, group, head_width)
    scores = (
        jnp.einsum(
            "bkgd,bskd->bkgs",
            self_query_rows,
            self_cache[..., :head_width],
            preferred_element_type=jnp.float32,
        )
        * score_scale
    )
    live = jnp.arange(self_cache.shape[1], dtype=jnp.int32)[None, :] < cache_len[:, None]
    weight = jnp.where(live[:, None, None, :], jnp.exp(scores), jnp.float32(0.0))
    fresh_weight = jnp.exp(
        jnp.einsum(
            "ptwe,pte->ptw",
            self_query_rows,
            fresh_key_value[..., :head_width],
            preferred_element_type=jnp.float32,
        )
        * score_scale
    )
    total = jnp.sum(weight, axis=-1) + fresh_weight
    numer = jnp.einsum(
        "bkgs,bskd->bkgd",
        weight.astype(jnp.bfloat16),
        self_cache[..., head_width:],
        preferred_element_type=jnp.float32,
    )
    numer = numer + fresh_weight.astype(jnp.bfloat16).astype(jnp.float32)[
        ..., None
    ] * fresh_key_value[:, :, None, head_width:].astype(jnp.float32)
    self_out = (
        (numer / total[..., None]).astype(jnp.bfloat16).reshape(req_count, sq_heads, head_width)
    )

    owner_match = (owners == me_rep).astype(jnp.int32)
    rank_all = jnp.cumsum(owner_match, axis=1, dtype=jnp.int32) - owner_match
    slot_ids = jnp.arange(slot_cap, dtype=jnp.int32)
    chosen = owner_match[:, None, :] * (rank_all[:, None, :] == slot_ids[None, :, None]).astype(
        jnp.int32
    )
    slot_live = jnp.sum(chosen, axis=-1, dtype=jnp.int32)
    slot_req = jnp.sum(chosen * requests[:, None, :], axis=-1, dtype=jnp.int32)
    slot_tag = jnp.where(slot_live > 0, slot_req, -1)
    row_tag = jnp.broadcast_to(slot_tag[:, :, None], (n_rep, slot_cap, patches)).reshape(
        slot_all * patches
    )
    cross_out = attend(row_tag, cross_query, arrived.reshape(slot_all * patches, width2))
    return (cross_out, self_out)


def solution(mesh):
    return jax.shard_map(
        local,
        mesh=mesh,
        in_specs=(
            P("replica", None, "tensor"),
            P("tensor", None, None),
            P(),
            P(),
            P("replica", "tensor", None),
            P("replica", "tensor", None),
            P("replica", None, "tensor", None),
            P("replica", "tensor", None),
            P("replica"),
        ),
        out_specs=(P("replica", "tensor", None), P("replica", "tensor", None)),
        check_vma=False,
    )
```

```python
import math

import jax
import jax.numpy as jnp
from jax import lax
from jax.experimental import pallas as pl
from jax.experimental.pallas import tpu as pltpu
from jax.sharding import PartitionSpec as P


CHUNKS = 4
FEATURES_AT = 1


def head_order(count, outward):
    ten = lax.axis_index("tensor")
    n_ten = lax.axis_size("tensor")
    if outward:
        odd = lax.rem(ten + lax.axis_index("replica"), 2)
        ten = lax.rem(ten + jnp.where(odd == 0, 1, n_ten - 1), n_ten)
    side = lax.rem(ten, 2)
    return [lax.rem(ten // 2 + apart, count) * 2 + side for apart in (2, 1, count - 1, 0)]


def multiply(flat, wide, outward, out_a, out_b):
    count = out_a.shape[0]
    for i, head in enumerate(head_order(2 * count, outward)):
        product = jnp.dot(flat[...], wide[head], preferred_element_type=jnp.float32)
        if i < count:
            out_a[i] = product.astype(jnp.bfloat16)
        else:
            out_b[i - count] = product.astype(jnp.bfloat16)


def leave_body(features_ref, weight_ref, out_a, out_b, flat, wide, raw, feat, sem):
    step = weight_ref.shape[0] // CHUNKS
    parts = [pl.ds(k * step, step) for k in range(CHUNKS)]
    loads = [
        pltpu.make_async_copy(weight_ref.at[part], raw.at[part], sem.at[k])
        for k, part in enumerate(parts)
    ]
    loads.insert(FEATURES_AT, pltpu.make_async_copy(features_ref, feat, sem.at[CHUNKS]))
    for load in loads:
        load.start()
    first = loads.pop(FEATURES_AT)
    for k, part in enumerate(parts):
        loads[k].wait()
        wide[:, part, :] = jnp.swapaxes(raw[part], 0, 1)
        if k == min(FEATURES_AT, CHUNKS - 1):
            first.wait()
            flat[...] = feat[...].reshape(flat.shape)
    multiply(flat, wide, True, out_a, out_b)


def stay_body(flat, wide, out_a, out_b):
    multiply(flat, wide, False, out_a, out_b)


def leave(features, weight):
    images, patches, block = features.shape
    heads, width = weight.shape[1:]
    rows = images * patches
    count = heads // 4
    return pl.pallas_call(
        leave_body,
        in_specs=[pl.BlockSpec(memory_space=pltpu.HBM)] * 2,
        out_specs=(pl.BlockSpec(memory_space=pltpu.VMEM),) * 4,
        out_shape=(
            jax.ShapeDtypeStruct((count, rows, width), jnp.bfloat16),
            jax.ShapeDtypeStruct((count, rows, width), jnp.bfloat16),
            jax.ShapeDtypeStruct((rows, block), jnp.bfloat16),
            jax.ShapeDtypeStruct((heads, block, width), jnp.bfloat16),
        ),
        scratch_shapes=[
            pltpu.VMEM((block, heads, width), jnp.bfloat16),
            pltpu.VMEM((images, patches, block), jnp.bfloat16),
            pltpu.SemaphoreType.DMA((CHUNKS + 1,)),
        ],
        compiler_params=pltpu.CompilerParams(vmem_limit_bytes=32 << 20),
    )(
        pltpu.with_memory_space_constraint(features, pltpu.HBM),
        pltpu.with_memory_space_constraint(weight, pltpu.HBM),
    )


def stay(flat, wide):
    rows = flat.shape[0]
    heads, _, width = wide.shape
    part = jax.ShapeDtypeStruct((heads // 4, rows, width), jnp.bfloat16)
    return pl.pallas_call(
        stay_body,
        in_specs=[pl.BlockSpec(memory_space=pltpu.VMEM)] * 2,
        out_specs=(pl.BlockSpec(memory_space=pltpu.VMEM),) * 2,
        out_shape=(part, part),
        compiler_params=pltpu.CompilerParams(vmem_limit_bytes=32 << 20),
    )(*[pltpu.with_memory_space_constraint(x, pltpu.VMEM) for x in (flat, wide)])


def place_body(slot_ref, kept_ref, got_ref, a_ref, b_ref, c_ref, out_ref):
    own = kept_ref[1].astype(jnp.float32) + got_ref[1].astype(jnp.float32)
    for ref in (a_ref, b_ref, c_ref):
        own = own + ref[...].astype(jnp.float32)
    slots = lax.broadcasted_iota(jnp.int32, (out_ref.shape[0], own.shape[0]), 0)
    placing = (slots == slot_ref[...]).astype(jnp.float32).astype(jnp.bfloat16)
    out_ref[...] = jnp.dot(
        placing, own.astype(jnp.bfloat16), preferred_element_type=jnp.float32
    ).astype(jnp.bfloat16)


def place(row_slot, kept, got, arrivals, slot_rows):
    rows, width = arrivals[0].shape
    operands = (row_slot.reshape(1, rows), kept, got, *arrivals)
    whole = pl.BlockSpec(memory_space=pltpu.VMEM)
    return pl.pallas_call(
        place_body,
        in_specs=[whole] * len(operands),
        out_specs=whole,
        out_shape=jax.ShapeDtypeStruct((slot_rows, width), jnp.bfloat16),
    )(*[pltpu.with_memory_space_constraint(x, pltpu.VMEM) for x in operands])


def attend_body(tag_ref, query_ref, kv_ref, out_ref):
    count, group, head_width = query_ref.shape
    slot_rows = kv_ref.shape[0]
    scale = 1.0 / math.sqrt(head_width)
    raw = kv_ref[:, :head_width].astype(jnp.float32)
    keys = (
        raw * lax.rsqrt(jnp.mean(raw * raw, axis=-1, keepdims=True) + 1e-05)
    ).astype(jnp.bfloat16)
    query = query_ref[...].reshape(count * group, head_width)
    scores = lax.dot_general(
        query, keys, (((1,), (1,)), ((), ())), preferred_element_type=jnp.float32
    )
    request = lax.broadcasted_iota(jnp.int32, (count * group, slot_rows), 0) // group
    mask = request == tag_ref[...]
    weight = jnp.where(mask, jnp.exp(scores * scale), 0.0)
    total = jnp.sum(weight, axis=-1, keepdims=True)
    present = jnp.max(mask.astype(jnp.float32), axis=-1, keepdims=True) > 0.0
    numer = jnp.dot(
        weight.astype(jnp.bfloat16), kv_ref[:, head_width:], preferred_element_type=jnp.float32
    )
    result = jnp.where(present, numer / jnp.where(present, total, 1.0), 0.0)
    out_ref[...] = result.astype(jnp.bfloat16).reshape(out_ref.shape)


def attend(row_tag, query, kv):
    operands = (row_tag.reshape(1, kv.shape[0]), query, kv)
    return pl.pallas_call(
        attend_body,
        in_specs=[pl.BlockSpec(memory_space=pltpu.VMEM)] * 3,
        out_shape=jax.ShapeDtypeStruct(query.shape, jnp.bfloat16),
    )(*[pltpu.with_memory_space_constraint(x, pltpu.VMEM) for x in operands])


def local(
    features,
    kv_weight,
    image_owner,
    image_request,
    cross_query,
    self_query,
    self_cache,
    fresh_key_value,
    cache_len,
):
    n_rep = lax.axis_size("replica")
    n_ten = lax.axis_size("tensor")
    me_rep = lax.axis_index("replica")
    images, patches, block = features.shape
    kvh_all, width2 = kv_weight.shape[1:]
    head_width = width2 // 2
    score_scale = 1.0 / math.sqrt(head_width)
    slot_cap = max(2, 2 * images // n_rep)
    slot_all = n_rep * slot_cap
    rows = images * patches
    req_count, sq_heads, _ = self_query.shape
    kvh_local = self_cache.shape[2]
    group = sq_heads // kvh_local

    quarter = kvh_all // 2
    neighbours = []
    for r in range(n_rep):
        for z in range(n_ten):
            step = 1 if (z + r) % 2 == 0 else -1
            neighbours.append((r * n_ten + z, r * n_ten + (z + step) % n_ten))
    both = ("replica", "tensor")
    sent_a, sent_b, flat, wide = leave(features, kv_weight)
    got_a = lax.ppermute(sent_a, both, neighbours)
    got_b = lax.ppermute(sent_b, both, neighbours)
    kept_a, kept_b = stay(flat, wide)
    pair_a = (kept_a.astype(jnp.float32) + got_a.astype(jnp.float32)).astype(jnp.bfloat16)
    pair_b = (kept_b[0].astype(jnp.float32) + got_b[0].astype(jnp.float32)).astype(jnp.bfloat16)
    arrivals = [
        lax.ppermute(outward, "tensor", [(z, (z + 2 * step) % n_ten) for z in range(n_ten)])
        for outward, step in ((pair_a[0], 2), (pair_a[1], 1), (pair_b, quarter - 1))
    ]

    owners = image_owner.reshape(n_rep, images)
    requests = image_request.reshape(n_rep, images)
    own_block = lax.dynamic_index_in_dim(owners, me_rep, 0, keepdims=False)
    positions = jnp.arange(images, dtype=jnp.int32)
    same_owner = own_block[:, None] == own_block[None, :]
    earlier = positions[:, None] > positions[None, :]
    rank = jnp.sum((same_owner & earlier).astype(jnp.int32), axis=1, dtype=jnp.int32)
    slot = own_block * slot_cap + rank
    row_slot = (slot[:, None] * patches + jnp.arange(patches, dtype=jnp.int32)[None, :]).reshape(rows)
    outgoing = place(row_slot, kept_b, got_b, arrivals, slot_all * patches)
    outgoing = outgoing.reshape(n_rep, slot_cap * patches, width2)
    arrived = lax.all_to_all(outgoing, "replica", split_axis=0, concat_axis=0, tiled=True)

    self_query_rows = self_query.reshape(req_count, kvh_local, group, head_width)
    scores = (
        jnp.einsum(
            "bkgd,bskd->bkgs",
            self_query_rows,
            self_cache[..., :head_width],
            preferred_element_type=jnp.float32,
        )
        * score_scale
    )
    live = jnp.arange(self_cache.shape[1], dtype=jnp.int32)[None, :] < cache_len[:, None]
    weight = jnp.where(live[:, None, None, :], jnp.exp(scores), jnp.float32(0.0))
    fresh_weight = jnp.exp(
        jnp.einsum(
            "ptwe,pte->ptw",
            self_query_rows,
            fresh_key_value[..., :head_width],
            preferred_element_type=jnp.float32,
        )
        * score_scale
    )
    total = jnp.sum(weight, axis=-1) + fresh_weight
    numer = jnp.einsum(
        "bkgs,bskd->bkgd",
        weight.astype(jnp.bfloat16),
        self_cache[..., head_width:],
        preferred_element_type=jnp.float32,
    )
    numer = numer + fresh_weight.astype(jnp.bfloat16).astype(jnp.float32)[
        ..., None
    ] * fresh_key_value[:, :, None, head_width:].astype(jnp.float32)
    self_out = (
        (numer / total[..., None]).astype(jnp.bfloat16).reshape(req_count, sq_heads, head_width)
    )

    owner_match = (owners == me_rep).astype(jnp.int32)
    rank_all = jnp.cumsum(owner_match, axis=1, dtype=jnp.int32) - owner_match
    slot_ids = jnp.arange(slot_cap, dtype=jnp.int32)
    chosen = owner_match[:, None, :] * (rank_all[:, None, :] == slot_ids[None, :, None]).astype(
        jnp.int32
    )
    slot_live = jnp.sum(chosen, axis=-1, dtype=jnp.int32)
    slot_req = jnp.sum(chosen * requests[:, None, :], axis=-1, dtype=jnp.int32)
    slot_tag = jnp.where(slot_live > 0, slot_req, -1)
    row_tag = jnp.broadcast_to(slot_tag[:, :, None], (n_rep, slot_cap, patches)).reshape(
        slot_all * patches
    )
    cross_out = attend(row_tag, cross_query, arrived.reshape(slot_all * patches, width2))
    return (cross_out, self_out)


def solution(mesh):
    return jax.shard_map(
        local,
        mesh=mesh,
        in_specs=(
            P("replica", None, "tensor"),
            P("tensor", None, None),
            P(),
            P(),
            P("replica", "tensor", None),
            P("replica", "tensor", None),
            P("replica", None, "tensor", None),
            P("replica", "tensor", None),
            P("replica"),
        ),
        out_specs=(P("replica", "tensor", None), P("replica", "tensor", None)),
        check_vma=False,
    )
```

```python
import math

import jax
import jax.numpy as jnp
from jax import lax
from jax.experimental import pallas as pl
from jax.experimental.pallas import tpu as pltpu
from jax.sharding import PartitionSpec as P


STEP = 256
EARLY = 2


def head_order(count, outward):
    ten = lax.axis_index("tensor")
    n_ten = lax.axis_size("tensor")
    if outward:
        odd = lax.rem(ten + lax.axis_index("replica"), 2)
        ten = lax.rem(ten + jnp.where(odd == 0, 1, n_ten - 1), n_ten)
    side = lax.rem(ten, 2)
    return [lax.rem(ten // 2 + apart, count) * 2 + side for apart in (2, 1, count - 1, 0)]


def project_body(features_ref, weight_ref, *refs):
    outs, (flat, wide, raw, feat, early, sem) = refs[:4], refs[4:]
    block = weight_ref.shape[0]
    places = [(out, i) for out in outs for i in range(out.shape[0])]
    parts = [pl.ds(lo, min(STEP, block - lo)) for lo in range(0, block, STEP)]
    first = pltpu.make_async_copy(features_ref, feat, sem.at[len(parts)])
    loads = [
        pltpu.make_async_copy(weight_ref.at[part], raw.at[part], sem.at[k])
        for k, part in enumerate(parts)
    ]
    loads[0].start()
    first.start()
    for load in loads[1:]:
        load.start()
    count = len(places) // 2
    heads = head_order(count, True) + head_order(count, False)
    cut = EARLY * STEP
    for k, part in enumerate(parts):
        loads[k].wait()
        wide[:, part, :] = jnp.swapaxes(raw[part], 0, 1)
        if k == 0:
            first.wait()
            flat[...] = feat[...].reshape(flat.shape)
        if k == EARLY - 1:
            for i, head in enumerate(heads):
                early[i] = jnp.dot(
                    flat[:, :cut], wide[head, :cut, :], preferred_element_type=jnp.float32
                )
    for i, head in enumerate(heads):
        late = jnp.dot(flat[:, cut:], wide[head, cut:, :], preferred_element_type=jnp.float32)
        out, at = places[i]
        out[at] = (early[i] + late).astype(jnp.bfloat16)


def project(features, weight):
    images, patches, block = features.shape
    heads, width = weight.shape[1:]
    rows = images * patches
    counts = (1, heads // 2 - 1) * 2
    copies = pl.cdiv(block, STEP)
    return pl.pallas_call(
        project_body,
        in_specs=[pl.BlockSpec(memory_space=pltpu.HBM)] * 2,
        out_specs=(pl.BlockSpec(memory_space=pltpu.VMEM),) * 4,
        out_shape=tuple(jax.ShapeDtypeStruct((n, rows, width), jnp.bfloat16) for n in counts),
        scratch_shapes=[
            pltpu.VMEM((rows, block), jnp.bfloat16),
            pltpu.VMEM((heads, block, width), jnp.bfloat16),
            pltpu.VMEM((block, heads, width), jnp.bfloat16),
            pltpu.VMEM((images, patches, block), jnp.bfloat16),
            pltpu.VMEM((heads, rows, width), jnp.float32),
            pltpu.SemaphoreType.DMA((copies + 1,)),
        ],
        compiler_params=pltpu.CompilerParams(vmem_limit_bytes=32 << 20),
    )(
        pltpu.with_memory_space_constraint(features, pltpu.HBM),
        pltpu.with_memory_space_constraint(weight, pltpu.HBM),
    )


def place_body(slot_ref, kept_ref, got_ref, a_ref, b_ref, c_ref, out_ref):
    own = kept_ref[...].astype(jnp.float32) + got_ref[...].astype(jnp.float32)
    for ref in (a_ref, b_ref, c_ref):
        own = own + ref[...].astype(jnp.float32)
    slots = lax.broadcasted_iota(jnp.int32, (out_ref.shape[0], own.shape[0]), 0)
    placing = (slots == slot_ref[...]).astype(jnp.float32).astype(jnp.bfloat16)
    out_ref[...] = jnp.dot(
        placing, own.astype(jnp.bfloat16), preferred_element_type=jnp.float32
    ).astype(jnp.bfloat16)


def place(row_slot, kept, got, arrivals, slot_rows):
    rows, width = arrivals[0].shape
    operands = (row_slot.reshape(1, rows), kept, got, *arrivals)
    whole = pl.BlockSpec(memory_space=pltpu.VMEM)
    return pl.pallas_call(
        place_body,
        in_specs=[whole] * len(operands),
        out_specs=whole,
        out_shape=jax.ShapeDtypeStruct((slot_rows, width), jnp.bfloat16),
    )(*[pltpu.with_memory_space_constraint(x, pltpu.VMEM) for x in operands])


def attend_body(tag_ref, query_ref, kv_ref, out_ref):
    count, group, head_width = query_ref.shape
    slot_rows = kv_ref.shape[0]
    scale = 1.0 / math.sqrt(head_width)
    raw = kv_ref[:, :head_width].astype(jnp.float32)
    keys = (
        raw * lax.rsqrt(jnp.mean(raw * raw, axis=-1, keepdims=True) + 1e-05)
    ).astype(jnp.bfloat16)
    query = query_ref[...].reshape(count * group, head_width)
    scores = lax.dot_general(
        query, keys, (((1,), (1,)), ((), ())), preferred_element_type=jnp.float32
    )
    request = lax.broadcasted_iota(jnp.int32, (count * group, slot_rows), 0) // group
    mask = request == tag_ref[...]
    weight = jnp.where(mask, jnp.exp(scores * scale), 0.0)
    total = jnp.sum(weight, axis=-1, keepdims=True)
    present = jnp.max(mask.astype(jnp.float32), axis=-1, keepdims=True) > 0.0
    numer = jnp.dot(
        weight.astype(jnp.bfloat16), kv_ref[:, head_width:], preferred_element_type=jnp.float32
    )
    result = jnp.where(present, numer / jnp.where(present, total, 1.0), 0.0)
    out_ref[...] = result.astype(jnp.bfloat16).reshape(out_ref.shape)


def attend(row_tag, query, kv):
    operands = (row_tag.reshape(1, kv.shape[0]), query, kv)
    return pl.pallas_call(
        attend_body,
        in_specs=[pl.BlockSpec(memory_space=pltpu.VMEM)] * 3,
        out_shape=jax.ShapeDtypeStruct(query.shape, jnp.bfloat16),
    )(*[pltpu.with_memory_space_constraint(x, pltpu.VMEM) for x in operands])


def local(
    features,
    kv_weight,
    image_owner,
    image_request,
    cross_query,
    self_query,
    self_cache,
    fresh_key_value,
    cache_len,
):
    n_rep = lax.axis_size("replica")
    n_ten = lax.axis_size("tensor")
    me_rep = lax.axis_index("replica")
    images, patches, _ = features.shape
    kvh_all, width2 = kv_weight.shape[1:]
    head_width = width2 // 2
    score_scale = 1.0 / math.sqrt(head_width)
    slot_cap = max(2, 2 * images // n_rep)
    slot_all = n_rep * slot_cap
    rows = images * patches
    req_count, sq_heads, _ = self_query.shape
    kvh_local = self_cache.shape[2]
    group = sq_heads // kvh_local

    quarter = kvh_all // 2
    neighbours = []
    for r in range(n_rep):
        for z in range(n_ten):
            step = 1 if (z + r) % 2 == 0 else -1
            neighbours.append((r * n_ten + z, r * n_ten + (z + step) % n_ten))
    both = ("replica", "tensor")
    sent_a, sent_b, kept_a, kept_b = project(features, kv_weight)
    got_a = lax.ppermute(sent_a, both, neighbours)
    got_b = lax.ppermute(sent_b, both, neighbours)

    def onward(kept, got, step):
        outward = (kept.astype(jnp.float32) + got.astype(jnp.float32)).astype(jnp.bfloat16)
        return lax.ppermute(outward, "tensor", [(z, (z + 2 * step) % n_ten) for z in range(n_ten)])

    arrivals = (
        onward(kept_a[0], got_a[0], 2),
        onward(kept_b[0], got_b[0], 1),
        onward(kept_b[1], got_b[1], quarter - 1),
    )

    owners = image_owner.reshape(n_rep, images)
    requests = image_request.reshape(n_rep, images)
    own_block = lax.dynamic_index_in_dim(owners, me_rep, 0, keepdims=False)
    positions = jnp.arange(images, dtype=jnp.int32)
    same_owner = own_block[:, None] == own_block[None, :]
    earlier = positions[:, None] > positions[None, :]
    rank = jnp.sum((same_owner & earlier).astype(jnp.int32), axis=1, dtype=jnp.int32)
    slot = own_block * slot_cap + rank
    row_slot = (slot[:, None] * patches + jnp.arange(patches, dtype=jnp.int32)[None, :]).reshape(rows)
    outgoing = place(row_slot, kept_b[2], got_b[2], arrivals, slot_all * patches)
    outgoing = outgoing.reshape(n_rep, slot_cap * patches, width2)
    arrived = lax.all_to_all(outgoing, "replica", split_axis=0, concat_axis=0, tiled=True)

    self_query_rows = self_query.reshape(req_count, kvh_local, group, head_width)
    scores = (
        jnp.einsum(
            "bkgd,bskd->bkgs",
            self_query_rows,
            self_cache[..., :head_width],
            preferred_element_type=jnp.float32,
        )
        * score_scale
    )
    live = jnp.arange(self_cache.shape[1], dtype=jnp.int32)[None, :] < cache_len[:, None]
    weight = jnp.where(live[:, None, None, :], jnp.exp(scores), jnp.float32(0.0))
    fresh_weight = jnp.exp(
        jnp.einsum(
            "ptwe,pte->ptw",
            self_query_rows,
            fresh_key_value[..., :head_width],
            preferred_element_type=jnp.float32,
        )
        * score_scale
    )
    total = jnp.sum(weight, axis=-1) + fresh_weight
    numer = jnp.einsum(
        "bkgs,bskd->bkgd",
        weight.astype(jnp.bfloat16),
        self_cache[..., head_width:],
        preferred_element_type=jnp.float32,
    )
    numer = numer + fresh_weight.astype(jnp.bfloat16).astype(jnp.float32)[
        ..., None
    ] * fresh_key_value[:, :, None, head_width:].astype(jnp.float32)
    self_out = (
        (numer / total[..., None]).astype(jnp.bfloat16).reshape(req_count, sq_heads, head_width)
    )

    owner_match = (owners == me_rep).astype(jnp.int32)
    rank_all = jnp.cumsum(owner_match, axis=1, dtype=jnp.int32) - owner_match
    slot_ids = jnp.arange(slot_cap, dtype=jnp.int32)
    chosen = owner_match[:, None, :] * (rank_all[:, None, :] == slot_ids[None, :, None]).astype(
        jnp.int32
    )
    slot_live = jnp.sum(chosen, axis=-1, dtype=jnp.int32)
    slot_req = jnp.sum(chosen * requests[:, None, :], axis=-1, dtype=jnp.int32)
    slot_tag = jnp.where(slot_live > 0, slot_req, -1)
    row_tag = jnp.broadcast_to(slot_tag[:, :, None], (n_rep, slot_cap, patches)).reshape(
        slot_all * patches
    )
    cross_out = attend(row_tag, cross_query, arrived.reshape(slot_all * patches, width2))
    return (cross_out, self_out)


def solution(mesh):
    return jax.shard_map(
        local,
        mesh=mesh,
        in_specs=(
            P("replica", None, "tensor"),
            P("tensor", None, None),
            P(),
            P(),
            P("replica", "tensor", None),
            P("replica", "tensor", None),
            P("replica", None, "tensor", None),
            P("replica", "tensor", None),
            P("replica"),
        ),
        out_specs=(P("replica", "tensor", None), P("replica", "tensor", None)),
        check_vma=False,
    )
```

```python
import math

import jax
import jax.numpy as jnp
from jax import lax
from jax.experimental import pallas as pl
from jax.experimental.pallas import tpu as pltpu
from jax.sharding import PartitionSpec as P


STEP = 256
EARLY = 2


def head_order(count, outward):
    ten = lax.axis_index("tensor")
    n_ten = lax.axis_size("tensor")
    if outward:
        odd = lax.rem(ten + lax.axis_index("replica"), 2)
        ten = lax.rem(ten + jnp.where(odd == 0, 1, n_ten - 1), n_ten)
    side = lax.rem(ten, 2)
    return [lax.rem(ten // 2 + apart, count) * 2 + side for apart in (2, 1, count - 1, 0)]


def project_body(features_ref, weight_ref, *refs):
    outs, (flat, wide, raw, feat, early, sem) = refs[:4], refs[4:]
    block = weight_ref.shape[0]
    places = [(out, i) for out in outs for i in range(out.shape[0])]
    parts = [pl.ds(lo, min(STEP, block - lo)) for lo in range(0, block, STEP)]
    first = pltpu.make_async_copy(features_ref, feat, sem.at[len(parts)])
    loads = [
        pltpu.make_async_copy(weight_ref.at[part], raw.at[part], sem.at[k])
        for k, part in enumerate(parts)
    ]
    loads[0].start()
    first.start()
    for load in loads[1:]:
        load.start()
    count = len(places) // 2
    heads = head_order(count, True) + head_order(count, False)
    cut = EARLY * STEP
    for k, part in enumerate(parts):
        loads[k].wait()
        wide[:, part, :] = jnp.swapaxes(raw[part], 0, 1)
        if k == 0:
            first.wait()
            flat[...] = feat[...].reshape(flat.shape)
        if k == EARLY - 1:
            for i, head in enumerate(heads):
                early[i] = jnp.dot(
                    flat[:, :cut], wide[head, :cut, :], preferred_element_type=jnp.float32
                )
    for i, head in enumerate(heads):
        late = jnp.dot(flat[:, cut:], wide[head, cut:, :], preferred_element_type=jnp.float32)
        out, at = places[i]
        out[at] = (early[i] + late).astype(jnp.bfloat16)


def project(features, weight):
    images, patches, block = features.shape
    heads, width = weight.shape[1:]
    rows = images * patches
    counts = (1, heads // 2 - 1) * 2
    copies = pl.cdiv(block, STEP)
    return pl.pallas_call(
        project_body,
        in_specs=[pl.BlockSpec(memory_space=pltpu.HBM)] * 2,
        out_specs=(pl.BlockSpec(memory_space=pltpu.VMEM),) * 4,
        out_shape=tuple(jax.ShapeDtypeStruct((n, rows, width), jnp.bfloat16) for n in counts),
        scratch_shapes=[
            pltpu.VMEM((rows, block), jnp.bfloat16),
            pltpu.VMEM((heads, block, width), jnp.bfloat16),
            pltpu.VMEM((block, heads, width), jnp.bfloat16),
            pltpu.VMEM((images, patches, block), jnp.bfloat16),
            pltpu.VMEM((heads, rows, width), jnp.float32),
            pltpu.SemaphoreType.DMA((copies + 1,)),
        ],
        compiler_params=pltpu.CompilerParams(vmem_limit_bytes=32 << 20),
    )(
        pltpu.with_memory_space_constraint(features, pltpu.HBM),
        pltpu.with_memory_space_constraint(weight, pltpu.HBM),
    )


def place_body(slot_ref, kept_ref, got_ref, a_ref, b_ref, c_ref, out_ref):
    own = kept_ref[...].astype(jnp.float32) + got_ref[...].astype(jnp.float32)
    for ref in (a_ref, b_ref, c_ref):
        own = own + ref[...].astype(jnp.float32)
    slots = lax.broadcasted_iota(jnp.int32, (out_ref.shape[0], own.shape[0]), 0)
    placing = (slots == slot_ref[...]).astype(jnp.float32).astype(jnp.bfloat16)
    out_ref[...] = jnp.dot(
        placing, own.astype(jnp.bfloat16), preferred_element_type=jnp.float32
    ).astype(jnp.bfloat16)


def place(row_slot, kept, got, arrivals, slot_rows):
    rows, width = arrivals[0].shape
    operands = (row_slot.reshape(1, rows), kept, got, *arrivals)
    whole = pl.BlockSpec(memory_space=pltpu.VMEM)
    return pl.pallas_call(
        place_body,
        in_specs=[whole] * len(operands),
        out_specs=whole,
        out_shape=jax.ShapeDtypeStruct((slot_rows, width), jnp.bfloat16),
    )(*[pltpu.with_memory_space_constraint(x, pltpu.VMEM) for x in operands])


def attend_body(tag_ref, query_ref, kv_ref, out_ref):
    count, group, head_width = query_ref.shape
    slot_rows = kv_ref.shape[0]
    scale = 1.0 / math.sqrt(head_width)
    raw = kv_ref[:, :head_width].astype(jnp.float32)
    keys = (
        raw * lax.rsqrt(jnp.mean(raw * raw, axis=-1, keepdims=True) + 1e-05)
    ).astype(jnp.bfloat16)
    query = query_ref[...].reshape(count * group, head_width)
    scores = lax.dot_general(
        query, keys, (((1,), (1,)), ((), ())), preferred_element_type=jnp.float32
    )
    request = lax.broadcasted_iota(jnp.int32, (count * group, slot_rows), 0) // group
    mask = request == tag_ref[...]
    weight = jnp.where(mask, jnp.exp(scores * scale), 0.0)
    total = jnp.sum(weight, axis=-1, keepdims=True)
    present = jnp.max(mask.astype(jnp.float32), axis=-1, keepdims=True) > 0.0
    numer = jnp.dot(
        weight.astype(jnp.bfloat16), kv_ref[:, head_width:], preferred_element_type=jnp.float32
    )
    result = jnp.where(present, numer / jnp.where(present, total, 1.0), 0.0)
    out_ref[...] = result.astype(jnp.bfloat16).reshape(out_ref.shape)


def attend(row_tag, query, kv):
    operands = (row_tag.reshape(1, kv.shape[0]), query, kv)
    return pl.pallas_call(
        attend_body,
        in_specs=[pl.BlockSpec(memory_space=pltpu.VMEM)] * 3,
        out_shape=jax.ShapeDtypeStruct(query.shape, jnp.bfloat16),
    )(*[pltpu.with_memory_space_constraint(x, pltpu.VMEM) for x in operands])


def local(
    features,
    kv_weight,
    image_owner,
    image_request,
    cross_query,
    self_query,
    self_cache,
    fresh_key_value,
    cache_len,
):
    n_rep = lax.axis_size("replica")
    n_ten = lax.axis_size("tensor")
    me_rep = lax.axis_index("replica")
    images, patches, _ = features.shape
    kvh_all, width2 = kv_weight.shape[1:]
    head_width = width2 // 2
    score_scale = 1.0 / math.sqrt(head_width)
    slot_cap = max(2, 2 * images // n_rep)
    slot_all = n_rep * slot_cap
    rows = images * patches
    req_count, sq_heads, _ = self_query.shape
    kvh_local = self_cache.shape[2]
    group = sq_heads // kvh_local

    quarter = kvh_all // 2
    neighbours = []
    for r in range(n_rep):
        for z in range(n_ten):
            step = 1 if (z + r) % 2 == 0 else -1
            neighbours.append((r * n_ten + z, r * n_ten + (z + step) % n_ten))
    both = ("replica", "tensor")
    sent_a, sent_b, kept_a, kept_b = project(features, kv_weight)
    got_a = lax.ppermute(sent_a, both, neighbours)
    got_b = lax.ppermute(sent_b, both, neighbours)
    *later, got_b = lax.optimization_barrier(
        (
            image_owner,
            image_request,
            cross_query,
            self_query,
            self_cache,
            fresh_key_value,
            cache_len,
            got_b,
        )
    )
    image_owner, image_request, cross_query, self_query, *later = later
    self_cache, fresh_key_value, cache_len = later

    def onward(kept, got, step):
        outward = (kept.astype(jnp.float32) + got.astype(jnp.float32)).astype(jnp.bfloat16)
        return lax.ppermute(outward, "tensor", [(z, (z + 2 * step) % n_ten) for z in range(n_ten)])

    arrivals = (
        onward(kept_a[0], got_a[0], 2),
        onward(kept_b[0], got_b[0], 1),
        onward(kept_b[1], got_b[1], quarter - 1),
    )

    owners = image_owner.reshape(n_rep, images)
    requests = image_request.reshape(n_rep, images)
    own_block = lax.dynamic_index_in_dim(owners, me_rep, 0, keepdims=False)
    positions = jnp.arange(images, dtype=jnp.int32)
    same_owner = own_block[:, None] == own_block[None, :]
    earlier = positions[:, None] > positions[None, :]
    rank = jnp.sum((same_owner & earlier).astype(jnp.int32), axis=1, dtype=jnp.int32)
    slot = own_block * slot_cap + rank
    row_slot = (slot[:, None] * patches + jnp.arange(patches, dtype=jnp.int32)[None, :]).reshape(rows)
    outgoing = place(row_slot, kept_b[2], got_b[2], arrivals, slot_all * patches)
    outgoing = outgoing.reshape(n_rep, slot_cap * patches, width2)
    arrived = lax.all_to_all(outgoing, "replica", split_axis=0, concat_axis=0, tiled=True)

    self_query_rows = self_query.reshape(req_count, kvh_local, group, head_width)
    scores = (
        jnp.einsum(
            "bkgd,bskd->bkgs",
            self_query_rows,
            self_cache[..., :head_width],
            preferred_element_type=jnp.float32,
        )
        * score_scale
    )
    live = jnp.arange(self_cache.shape[1], dtype=jnp.int32)[None, :] < cache_len[:, None]
    weight = jnp.where(live[:, None, None, :], jnp.exp(scores), jnp.float32(0.0))
    fresh_weight = jnp.exp(
        jnp.einsum(
            "ptwe,pte->ptw",
            self_query_rows,
            fresh_key_value[..., :head_width],
            preferred_element_type=jnp.float32,
        )
        * score_scale
    )
    total = jnp.sum(weight, axis=-1) + fresh_weight
    numer = jnp.einsum(
        "bkgs,bskd->bkgd",
        weight.astype(jnp.bfloat16),
        self_cache[..., head_width:],
        preferred_element_type=jnp.float32,
    )
    numer = numer + fresh_weight.astype(jnp.bfloat16).astype(jnp.float32)[
        ..., None
    ] * fresh_key_value[:, :, None, head_width:].astype(jnp.float32)
    self_out = (
        (numer / total[..., None]).astype(jnp.bfloat16).reshape(req_count, sq_heads, head_width)
    )

    owner_match = (owners == me_rep).astype(jnp.int32)
    rank_all = jnp.cumsum(owner_match, axis=1, dtype=jnp.int32) - owner_match
    slot_ids = jnp.arange(slot_cap, dtype=jnp.int32)
    chosen = owner_match[:, None, :] * (rank_all[:, None, :] == slot_ids[None, :, None]).astype(
        jnp.int32
    )
    slot_live = jnp.sum(chosen, axis=-1, dtype=jnp.int32)
    slot_req = jnp.sum(chosen * requests[:, None, :], axis=-1, dtype=jnp.int32)
    slot_tag = jnp.where(slot_live > 0, slot_req, -1)
    row_tag = jnp.broadcast_to(slot_tag[:, :, None], (n_rep, slot_cap, patches)).reshape(
        slot_all * patches
    )
    cross_out = attend(row_tag, cross_query, arrived.reshape(slot_all * patches, width2))
    return (cross_out, self_out)


def solution(mesh):
    return jax.shard_map(
        local,
        mesh=mesh,
        in_specs=(
            P("replica", None, "tensor"),
            P("tensor", None, None),
            P(),
            P(),
            P("replica", "tensor", None),
            P("replica", "tensor", None),
            P("replica", None, "tensor", None),
            P("replica", "tensor", None),
            P("replica"),
        ),
        out_specs=(P("replica", "tensor", None), P("replica", "tensor", None)),
        check_vma=False,
    )
```

```python
import math

import jax
import jax.numpy as jnp
from jax import lax
from jax.experimental import pallas as pl
from jax.experimental.pallas import tpu as pltpu
from jax.sharding import PartitionSpec as P


STEP = 256
EARLY = 2


def head_order(count, outward):
    ten = lax.axis_index("tensor")
    n_ten = lax.axis_size("tensor")
    if outward:
        odd = lax.rem(ten + lax.axis_index("replica"), 2)
        ten = lax.rem(ten + jnp.where(odd == 0, 1, n_ten - 1), n_ten)
    side = lax.rem(ten, 2)
    return [lax.rem(ten // 2 + apart, count) * 2 + side for apart in (2, 1, count - 1, 0)]


def project_body(features_ref, weight_ref, *refs):
    outs, (flat, wide, raw, feat, early, sem) = refs[:4], refs[4:]
    block = weight_ref.shape[0]
    places = [(out, i) for out in outs for i in range(out.shape[0])]
    parts = [pl.ds(lo, min(STEP, block - lo)) for lo in range(0, block, STEP)]
    first = pltpu.make_async_copy(features_ref, feat, sem.at[len(parts)])
    loads = [
        pltpu.make_async_copy(weight_ref.at[part], raw.at[part], sem.at[k])
        for k, part in enumerate(parts)
    ]
    loads[0].start()
    first.start()
    for load in loads[1:]:
        load.start()
    count = len(places) // 2
    heads = head_order(count, True) + head_order(count, False)
    cut = EARLY * STEP
    for k, part in enumerate(parts):
        loads[k].wait()
        wide[:, part, :] = jnp.swapaxes(raw[part], 0, 1)
        if k == 0:
            first.wait()
            flat[...] = feat[...].reshape(flat.shape)
        if k == EARLY - 1:
            for i, head in enumerate(heads):
                early[i] = jnp.dot(
                    flat[:, :cut], wide[head, :cut, :], preferred_element_type=jnp.float32
                )
    for i, head in enumerate(heads):
        late = jnp.dot(flat[:, cut:], wide[head, cut:, :], preferred_element_type=jnp.float32)
        out, at = places[i]
        out[at] = (early[i] + late).astype(jnp.bfloat16)


def project(features, weight):
    images, patches, block = features.shape
    heads, width = weight.shape[1:]
    rows = images * patches
    counts = (heads // 4,) * 4
    copies = pl.cdiv(block, STEP)
    return pl.pallas_call(
        project_body,
        in_specs=[pl.BlockSpec(memory_space=pltpu.HBM)] * 2,
        out_specs=(pl.BlockSpec(memory_space=pltpu.VMEM),) * 4,
        out_shape=tuple(jax.ShapeDtypeStruct((n, rows, width), jnp.bfloat16) for n in counts),
        scratch_shapes=[
            pltpu.VMEM((rows, block), jnp.bfloat16),
            pltpu.VMEM((heads, block, width), jnp.bfloat16),
            pltpu.VMEM((block, heads, width), jnp.bfloat16),
            pltpu.VMEM((images, patches, block), jnp.bfloat16),
            pltpu.VMEM((heads, rows, width), jnp.float32),
            pltpu.SemaphoreType.DMA((copies + 1,)),
        ],
        compiler_params=pltpu.CompilerParams(vmem_limit_bytes=32 << 20),
    )(
        pltpu.with_memory_space_constraint(features, pltpu.HBM),
        pltpu.with_memory_space_constraint(weight, pltpu.HBM),
    )


def place_body(slot_ref, kept_ref, got_ref, a_ref, b_ref, c_ref, out_ref):
    own = kept_ref[...].astype(jnp.float32) + got_ref[...].astype(jnp.float32)
    for ref in (a_ref, b_ref, c_ref):
        own = own + ref[...].astype(jnp.float32)
    slots = lax.broadcasted_iota(jnp.int32, (out_ref.shape[0], own.shape[0]), 0)
    placing = (slots == slot_ref[...]).astype(jnp.float32).astype(jnp.bfloat16)
    out_ref[...] = jnp.dot(
        placing, own.astype(jnp.bfloat16), preferred_element_type=jnp.float32
    ).astype(jnp.bfloat16)


def place(row_slot, kept, got, arrivals, slot_rows):
    rows, width = arrivals[0].shape
    operands = (row_slot.reshape(1, rows), kept, got, *arrivals)
    whole = pl.BlockSpec(memory_space=pltpu.VMEM)
    return pl.pallas_call(
        place_body,
        in_specs=[whole] * len(operands),
        out_specs=whole,
        out_shape=jax.ShapeDtypeStruct((slot_rows, width), jnp.bfloat16),
    )(*[pltpu.with_memory_space_constraint(x, pltpu.VMEM) for x in operands])


def attend_body(tag_ref, query_ref, kv_ref, out_ref):
    count, group, head_width = query_ref.shape
    slot_rows = kv_ref.shape[0]
    scale = 1.0 / math.sqrt(head_width)
    raw = kv_ref[:, :head_width].astype(jnp.float32)
    keys = (
        raw * lax.rsqrt(jnp.mean(raw * raw, axis=-1, keepdims=True) + 1e-05)
    ).astype(jnp.bfloat16)
    query = query_ref[...].reshape(count * group, head_width)
    scores = lax.dot_general(
        query, keys, (((1,), (1,)), ((), ())), preferred_element_type=jnp.float32
    )
    request = lax.broadcasted_iota(jnp.int32, (count * group, slot_rows), 0) // group
    mask = request == tag_ref[...]
    weight = jnp.where(mask, jnp.exp(scores * scale), 0.0)
    total = jnp.sum(weight, axis=-1, keepdims=True)
    present = jnp.max(mask.astype(jnp.float32), axis=-1, keepdims=True) > 0.0
    numer = jnp.dot(
        weight.astype(jnp.bfloat16), kv_ref[:, head_width:], preferred_element_type=jnp.float32
    )
    result = jnp.where(present, numer / jnp.where(present, total, 1.0), 0.0)
    out_ref[...] = result.astype(jnp.bfloat16).reshape(out_ref.shape)


def attend(row_tag, query, kv):
    operands = (row_tag.reshape(1, kv.shape[0]), query, kv)
    return pl.pallas_call(
        attend_body,
        in_specs=[pl.BlockSpec(memory_space=pltpu.VMEM)] * 3,
        out_shape=jax.ShapeDtypeStruct(query.shape, jnp.bfloat16),
    )(*[pltpu.with_memory_space_constraint(x, pltpu.VMEM) for x in operands])


def local(
    features,
    kv_weight,
    image_owner,
    image_request,
    cross_query,
    self_query,
    self_cache,
    fresh_key_value,
    cache_len,
):
    n_rep = lax.axis_size("replica")
    n_ten = lax.axis_size("tensor")
    me_rep = lax.axis_index("replica")
    images, patches, _ = features.shape
    kvh_all, width2 = kv_weight.shape[1:]
    head_width = width2 // 2
    score_scale = 1.0 / math.sqrt(head_width)
    slot_cap = max(2, 2 * images // n_rep)
    slot_all = n_rep * slot_cap
    rows = images * patches
    req_count, sq_heads, _ = self_query.shape
    kvh_local = self_cache.shape[2]
    group = sq_heads // kvh_local

    quarter = kvh_all // 2
    neighbours = []
    for r in range(n_rep):
        for z in range(n_ten):
            step = 1 if (z + r) % 2 == 0 else -1
            neighbours.append((r * n_ten + z, r * n_ten + (z + step) % n_ten))
    both = ("replica", "tensor")
    sent_a, sent_b, kept_a, kept_b = project(features, kv_weight)
    got_a = lax.ppermute(sent_a, both, neighbours)
    got_b = lax.ppermute(sent_b, both, neighbours)

    def onward(kept, got, step):
        outward = (kept.astype(jnp.float32) + got.astype(jnp.float32)).astype(jnp.bfloat16)
        return lax.ppermute(outward, "tensor", [(z, (z + 2 * step) % n_ten) for z in range(n_ten)])

    arrivals = (
        onward(kept_a[0], got_a[0], 2),
        onward(kept_a[1], got_a[1], 1),
        onward(kept_b[0], got_b[0], quarter - 1),
    )

    owners = image_owner.reshape(n_rep, images)
    requests = image_request.reshape(n_rep, images)
    own_block = lax.dynamic_index_in_dim(owners, me_rep, 0, keepdims=False)
    positions = jnp.arange(images, dtype=jnp.int32)
    same_owner = own_block[:, None] == own_block[None, :]
    earlier = positions[:, None] > positions[None, :]
    rank = jnp.sum((same_owner & earlier).astype(jnp.int32), axis=1, dtype=jnp.int32)
    slot = own_block * slot_cap + rank
    row_slot = (slot[:, None] * patches + jnp.arange(patches, dtype=jnp.int32)[None, :]).reshape(rows)
    outgoing = place(row_slot, kept_b[1], got_b[1], arrivals, slot_all * patches)
    outgoing = outgoing.reshape(n_rep, slot_cap * patches, width2)
    arrived = lax.all_to_all(outgoing, "replica", split_axis=0, concat_axis=0, tiled=True)

    self_query_rows = self_query.reshape(req_count, kvh_local, group, head_width)
    scores = (
        jnp.einsum(
            "bkgd,bskd->bkgs",
            self_query_rows,
            self_cache[..., :head_width],
            preferred_element_type=jnp.float32,
        )
        * score_scale
    )
    live = jnp.arange(self_cache.shape[1], dtype=jnp.int32)[None, :] < cache_len[:, None]
    weight = jnp.where(live[:, None, None, :], jnp.exp(scores), jnp.float32(0.0))
    fresh_weight = jnp.exp(
        jnp.einsum(
            "ptwe,pte->ptw",
            self_query_rows,
            fresh_key_value[..., :head_width],
            preferred_element_type=jnp.float32,
        )
        * score_scale
    )
    total = jnp.sum(weight, axis=-1) + fresh_weight
    numer = jnp.einsum(
        "bkgs,bskd->bkgd",
        weight.astype(jnp.bfloat16),
        self_cache[..., head_width:],
        preferred_element_type=jnp.float32,
    )
    numer = numer + fresh_weight.astype(jnp.bfloat16).astype(jnp.float32)[
        ..., None
    ] * fresh_key_value[:, :, None, head_width:].astype(jnp.float32)
    self_out = (
        (numer / total[..., None]).astype(jnp.bfloat16).reshape(req_count, sq_heads, head_width)
    )

    owner_match = (owners == me_rep).astype(jnp.int32)
    rank_all = jnp.cumsum(owner_match, axis=1, dtype=jnp.int32) - owner_match
    slot_ids = jnp.arange(slot_cap, dtype=jnp.int32)
    chosen = owner_match[:, None, :] * (rank_all[:, None, :] == slot_ids[None, :, None]).astype(
        jnp.int32
    )
    slot_live = jnp.sum(chosen, axis=-1, dtype=jnp.int32)
    slot_req = jnp.sum(chosen * requests[:, None, :], axis=-1, dtype=jnp.int32)
    slot_tag = jnp.where(slot_live > 0, slot_req, -1)
    row_tag = jnp.broadcast_to(slot_tag[:, :, None], (n_rep, slot_cap, patches)).reshape(
        slot_all * patches
    )
    cross_out = attend(row_tag, cross_query, arrived.reshape(slot_all * patches, width2))
    return (cross_out, self_out)


def solution(mesh):
    return jax.shard_map(
        local,
        mesh=mesh,
        in_specs=(
            P("replica", None, "tensor"),
            P("tensor", None, None),
            P(),
            P(),
            P("replica", "tensor", None),
            P("replica", "tensor", None),
            P("replica", None, "tensor", None),
            P("replica", "tensor", None),
            P("replica"),
        ),
        out_specs=(P("replica", "tensor", None), P("replica", "tensor", None)),
        check_vma=False,
    )
```

```python
import math

import jax
import jax.numpy as jnp
from jax import lax
from jax.experimental import pallas as pl
from jax.experimental.pallas import tpu as pltpu
from jax.sharding import PartitionSpec as P


STEP = 256
EARLY = 2


def head_order(count, outward):
    ten = lax.axis_index("tensor")
    n_ten = lax.axis_size("tensor")
    if outward:
        odd = lax.rem(ten + lax.axis_index("replica"), 2)
        ten = lax.rem(ten + jnp.where(odd == 0, 1, n_ten - 1), n_ten)
    side = lax.rem(ten, 2)
    return [lax.rem(ten // 2 + apart, count) * 2 + side for apart in (1, count - 1, 2, 0)]


def project_body(features_ref, weight_ref, *refs):
    outs, (flat, wide, raw, feat, early, sem) = refs[:4], refs[4:]
    block = weight_ref.shape[0]
    places = [(out, i) for out in outs for i in range(out.shape[0])]
    parts = [pl.ds(lo, min(STEP, block - lo)) for lo in range(0, block, STEP)]
    first = pltpu.make_async_copy(features_ref, feat, sem.at[len(parts)])
    loads = [
        pltpu.make_async_copy(weight_ref.at[part], raw.at[part], sem.at[k])
        for k, part in enumerate(parts)
    ]
    loads[0].start()
    first.start()
    for load in loads[1:]:
        load.start()
    count = len(places) // 2
    heads = head_order(count, True) + head_order(count, False)
    cut = EARLY * STEP
    for k, part in enumerate(parts):
        loads[k].wait()
        wide[:, part, :] = jnp.swapaxes(raw[part], 0, 1)
        if k == 0:
            first.wait()
            flat[...] = feat[...].reshape(flat.shape)
        if k == EARLY - 1:
            for i, head in enumerate(heads):
                early[i] = jnp.dot(
                    flat[:, :cut], wide[head, :cut, :], preferred_element_type=jnp.float32
                )
    for i, head in enumerate(heads):
        late = jnp.dot(flat[:, cut:], wide[head, cut:, :], preferred_element_type=jnp.float32)
        out, at = places[i]
        out[at] = (early[i] + late).astype(jnp.bfloat16)


def project(features, weight):
    images, patches, block = features.shape
    heads, width = weight.shape[1:]
    rows = images * patches
    counts = (heads // 4,) * 4
    copies = pl.cdiv(block, STEP)
    return pl.pallas_call(
        project_body,
        in_specs=[pl.BlockSpec(memory_space=pltpu.HBM)] * 2,
        out_specs=(pl.BlockSpec(memory_space=pltpu.VMEM),) * 4,
        out_shape=tuple(jax.ShapeDtypeStruct((n, rows, width), jnp.bfloat16) for n in counts),
        scratch_shapes=[
            pltpu.VMEM((rows, block), jnp.bfloat16),
            pltpu.VMEM((heads, block, width), jnp.bfloat16),
            pltpu.VMEM((block, heads, width), jnp.bfloat16),
            pltpu.VMEM((images, patches, block), jnp.bfloat16),
            pltpu.VMEM((heads, rows, width), jnp.float32),
            pltpu.SemaphoreType.DMA((copies + 1,)),
        ],
        compiler_params=pltpu.CompilerParams(vmem_limit_bytes=32 << 20),
    )(
        pltpu.with_memory_space_constraint(features, pltpu.HBM),
        pltpu.with_memory_space_constraint(weight, pltpu.HBM),
    )


def place_body(slot_ref, kept_ref, got_ref, a_ref, b_ref, c_ref, out_ref):
    own = kept_ref[...].astype(jnp.float32) + got_ref[...].astype(jnp.float32)
    for ref in (a_ref, b_ref, c_ref):
        own = own + ref[...].astype(jnp.float32)
    slots = lax.broadcasted_iota(jnp.int32, (out_ref.shape[0], own.shape[0]), 0)
    placing = (slots == slot_ref[...]).astype(jnp.float32).astype(jnp.bfloat16)
    out_ref[...] = jnp.dot(
        placing, own.astype(jnp.bfloat16), preferred_element_type=jnp.float32
    ).astype(jnp.bfloat16)


def place(row_slot, kept, got, arrivals, slot_rows):
    rows, width = arrivals[0].shape
    operands = (row_slot.reshape(1, rows), kept, got, *arrivals)
    whole = pl.BlockSpec(memory_space=pltpu.VMEM)
    return pl.pallas_call(
        place_body,
        in_specs=[whole] * len(operands),
        out_specs=whole,
        out_shape=jax.ShapeDtypeStruct((slot_rows, width), jnp.bfloat16),
    )(*[pltpu.with_memory_space_constraint(x, pltpu.VMEM) for x in operands])


def attend_body(tag_ref, query_ref, kv_ref, out_ref):
    count, group, head_width = query_ref.shape
    slot_rows = kv_ref.shape[0]
    scale = 1.0 / math.sqrt(head_width)
    raw = kv_ref[:, :head_width].astype(jnp.float32)
    keys = (
        raw * lax.rsqrt(jnp.mean(raw * raw, axis=-1, keepdims=True) + 1e-05)
    ).astype(jnp.bfloat16)
    query = query_ref[...].reshape(count * group, head_width)
    scores = lax.dot_general(
        query, keys, (((1,), (1,)), ((), ())), preferred_element_type=jnp.float32
    )
    request = lax.broadcasted_iota(jnp.int32, (count * group, slot_rows), 0) // group
    mask = request == tag_ref[...]
    weight = jnp.where(mask, jnp.exp(scores * scale), 0.0)
    total = jnp.sum(weight, axis=-1, keepdims=True)
    present = jnp.max(mask.astype(jnp.float32), axis=-1, keepdims=True) > 0.0
    numer = jnp.dot(
        weight.astype(jnp.bfloat16), kv_ref[:, head_width:], preferred_element_type=jnp.float32
    )
    result = jnp.where(present, numer / jnp.where(present, total, 1.0), 0.0)
    out_ref[...] = result.astype(jnp.bfloat16).reshape(out_ref.shape)


def attend(row_tag, query, kv):
    operands = (row_tag.reshape(1, kv.shape[0]), query, kv)
    return pl.pallas_call(
        attend_body,
        in_specs=[pl.BlockSpec(memory_space=pltpu.VMEM)] * 3,
        out_shape=jax.ShapeDtypeStruct(query.shape, jnp.bfloat16),
    )(*[pltpu.with_memory_space_constraint(x, pltpu.VMEM) for x in operands])


def local(
    features,
    kv_weight,
    image_owner,
    image_request,
    cross_query,
    self_query,
    self_cache,
    fresh_key_value,
    cache_len,
):
    n_rep = lax.axis_size("replica")
    n_ten = lax.axis_size("tensor")
    me_rep = lax.axis_index("replica")
    images, patches, _ = features.shape
    kvh_all, width2 = kv_weight.shape[1:]
    head_width = width2 // 2
    score_scale = 1.0 / math.sqrt(head_width)
    slot_cap = max(2, 2 * images // n_rep)
    slot_all = n_rep * slot_cap
    rows = images * patches
    req_count, sq_heads, _ = self_query.shape
    kvh_local = self_cache.shape[2]
    group = sq_heads // kvh_local

    quarter = kvh_all // 2
    neighbours = []
    for r in range(n_rep):
        for z in range(n_ten):
            step = 1 if (z + r) % 2 == 0 else -1
            neighbours.append((r * n_ten + z, r * n_ten + (z + step) % n_ten))
    both = ("replica", "tensor")
    sent_a, sent_b, kept_a, kept_b = project(features, kv_weight)
    got_a = lax.ppermute(sent_a, both, neighbours)
    got_b = lax.ppermute(sent_b, both, neighbours)

    def onward(kept, got, step):
        outward = (kept.astype(jnp.float32) + got.astype(jnp.float32)).astype(jnp.bfloat16)
        return lax.ppermute(outward, "tensor", [(z, (z + 2 * step) % n_ten) for z in range(n_ten)])

    arrivals = (
        onward(kept_a[0], got_a[0], 1),
        onward(kept_a[1], got_a[1], quarter - 1),
        onward(kept_b[0], got_b[0], 2),
    )

    owners = image_owner.reshape(n_rep, images)
    requests = image_request.reshape(n_rep, images)
    own_block = lax.dynamic_index_in_dim(owners, me_rep, 0, keepdims=False)
    positions = jnp.arange(images, dtype=jnp.int32)
    same_owner = own_block[:, None] == own_block[None, :]
    earlier = positions[:, None] > positions[None, :]
    rank = jnp.sum((same_owner & earlier).astype(jnp.int32), axis=1, dtype=jnp.int32)
    slot = own_block * slot_cap + rank
    row_slot = (slot[:, None] * patches + jnp.arange(patches, dtype=jnp.int32)[None, :]).reshape(rows)
    outgoing = place(row_slot, kept_b[1], got_b[1], arrivals, slot_all * patches)
    outgoing = outgoing.reshape(n_rep, slot_cap * patches, width2)
    arrived = lax.all_to_all(outgoing, "replica", split_axis=0, concat_axis=0, tiled=True)

    self_query_rows = self_query.reshape(req_count, kvh_local, group, head_width)
    scores = (
        jnp.einsum(
            "bkgd,bskd->bkgs",
            self_query_rows,
            self_cache[..., :head_width],
            preferred_element_type=jnp.float32,
        )
        * score_scale
    )
    live = jnp.arange(self_cache.shape[1], dtype=jnp.int32)[None, :] < cache_len[:, None]
    weight = jnp.where(live[:, None, None, :], jnp.exp(scores), jnp.float32(0.0))
    fresh_weight = jnp.exp(
        jnp.einsum(
            "ptwe,pte->ptw",
            self_query_rows,
            fresh_key_value[..., :head_width],
            preferred_element_type=jnp.float32,
        )
        * score_scale
    )
    total = jnp.sum(weight, axis=-1) + fresh_weight
    numer = jnp.einsum(
        "bkgs,bskd->bkgd",
        weight.astype(jnp.bfloat16),
        self_cache[..., head_width:],
        preferred_element_type=jnp.float32,
    )
    numer = numer + fresh_weight.astype(jnp.bfloat16).astype(jnp.float32)[
        ..., None
    ] * fresh_key_value[:, :, None, head_width:].astype(jnp.float32)
    self_out = (
        (numer / total[..., None]).astype(jnp.bfloat16).reshape(req_count, sq_heads, head_width)
    )

    owner_match = (owners == me_rep).astype(jnp.int32)
    rank_all = jnp.cumsum(owner_match, axis=1, dtype=jnp.int32) - owner_match
    slot_ids = jnp.arange(slot_cap, dtype=jnp.int32)
    chosen = owner_match[:, None, :] * (rank_all[:, None, :] == slot_ids[None, :, None]).astype(
        jnp.int32
    )
    slot_live = jnp.sum(chosen, axis=-1, dtype=jnp.int32)
    slot_req = jnp.sum(chosen * requests[:, None, :], axis=-1, dtype=jnp.int32)
    slot_tag = jnp.where(slot_live > 0, slot_req, -1)
    row_tag = jnp.broadcast_to(slot_tag[:, :, None], (n_rep, slot_cap, patches)).reshape(
        slot_all * patches
    )
    cross_out = attend(row_tag, cross_query, arrived.reshape(slot_all * patches, width2))
    return (cross_out, self_out)


def solution(mesh):
    return jax.shard_map(
        local,
        mesh=mesh,
        in_specs=(
            P("replica", None, "tensor"),
            P("tensor", None, None),
            P(),
            P(),
            P("replica", "tensor", None),
            P("replica", "tensor", None),
            P("replica", None, "tensor", None),
            P("replica", "tensor", None),
            P("replica"),
        ),
        out_specs=(P("replica", "tensor", None), P("replica", "tensor", None)),
        check_vma=False,
    )
```
